512 devices in a mesh: skill: 64 (over y_lo, x, z), tensor: 8 (over y_hi, core).
Axes of the slice: x: 4, y: 8 (y_hi: 4, y_lo: 2; y = y_hi * 2 + y_lo), z: 8, core: 2. Of those that a mesh axis runs over, the one named last changes fastest.
Arguments:
- stored_inputs: bfloat16 [64, 256, 8192], P('skill', None, 'tensor'), may hold values from -6 to 6
- stored_output_gradient: bfloat16 [64, 256, 15360], P('skill', None, 'tensor'), may hold values from -6 to 6
- training_token_index: int32 [64, 256], P('skill'), may hold values from 0 to 255
- validation_inputs: bfloat16 [64, 512, 8192], P('skill', None, 'tensor'), may hold values from -6 to 6
- validation_output_gradient: bfloat16 [64, 512, 15360], P('skill', None, 'tensor'), may hold values from -6 to 6
- validation_row_skill: int32 [64, 512], P('skill'), may hold values from 0 to 63
- adapter_down_init: bfloat16 [64, 8192, 64], P('skill', 'tensor'), may hold values from -0.0625 to 0.0625
Outputs:
- own_delta: float32 [64, 17], P('skill')
- other_delta: float32 [64, 17], P('skill')
The draws below stay inside these ranges and needn't reach their ends.
All inputs are finite; a program needn't handle non-finite values.
Results may differ from the reference program's by a relative error of at most 0.0042.
Values may be sent and summed in bfloat16 or wider, within the bound.
A program may use at most 64 MiB of HBM per device.

```python
import jax
import jax.numpy as jnp
from jax import lax

MODEL_WIDTH = 8192
FW = 15360
ADAPTER_RANK = 64
TRAIN = 256
VAL = 512
SKILL_COUNT = 64
REACH = 8
COLUMNS = 17


def draw_validation_row_skill(key, part):
    flip_key = jax.random.fold_in(key, 11)
    pick_key = jax.random.fold_in(key, 12)
    coin_flip = jax.random.randint(flip_key, (SKILL_COUNT, VAL), 0, 2)
    random_skill = jax.random.randint(pick_key, (SKILL_COUNT, VAL), 0, SKILL_COUNT)
    home_skill = lax.broadcasted_iota(jnp.int32, (SKILL_COUNT, VAL), 0)
    return jnp.where(coin_flip == 1, home_skill, random_skill).astype(jnp.int32)


def touch_ends(drawn, key, smallest, high):
    dims = drawn.shape
    spot = [jax.random.randint(jax.random.fold_in(key, axis), (), 0, dims[axis]) for axis in range(len(dims))]
    drawn = drawn.at[tuple(spot)].set(smallest)
    longest = dims.index(max(dims))
    spot[longest] = (spot[longest] + 1) % dims[longest]
    return drawn.at[tuple(spot)].set(high)


def steps_of(stream_key, dims, cuts, low, top_value):
    gain, own = 1.0, jax.random.fold_in(stream_key, 6)
    for dim, shards_of in cuts:
        steps = jnp.exp(jax.random.uniform(jax.random.fold_in(own, dim), (shards_of,), jnp.float32, low / len(cuts), top_value / len(cuts)))
        gain = gain * jnp.repeat(steps, dims[dim] // shards_of).reshape([-1 if axis == dim else 1 for axis in range(len(dims))])
    return gain


def scatter_about(stream_key, extent, deviation, limit, pieces=(), kind=jnp.bfloat16):
    factor_of = steps_of(stream_key, extent, pieces, -0.22, 0.18) if pieces else 1.0
    array = jax.random.normal(stream_key, extent, jnp.float32) * deviation * factor_of
    return jnp.minimum(jnp.maximum(array, -limit), limit).astype(kind)


def setup_inputs(seed: int = 0) -> dict:
    seeds = jax.random.split(jax.random.key(seed), 8)
    stored_inputs = scatter_about(seeds[0], (SKILL_COUNT, TRAIN, MODEL_WIDTH), 1.0, 6.0, ((0, 64), (2, 8)))
    stored_output_gradient = scatter_about(seeds[1], (SKILL_COUNT, TRAIN, FW), 1.0, 6.0, ((0, 64), (2, 8)))
    training_token_index = touch_ends(jax.random.randint(seeds[2], (SKILL_COUNT, TRAIN), 0, TRAIN), jax.random.fold_in(seeds[2], 1), 0, TRAIN - 1).astype(jnp.int32)
    validation_inputs = scatter_about(seeds[3], (SKILL_COUNT, VAL, MODEL_WIDTH), 1.0, 6.0, ((0, 64), (2, 8)))
    validation_output_gradient = scatter_about(seeds[4], (SKILL_COUNT, VAL, FW), 1.0, 6.0, ((0, 64), (2, 8)))
    validation_row_skill = draw_validation_row_skill(jax.random.fold_in(seeds[7], 71), 0)
    adapter_down_init = scatter_about(seeds[6], (SKILL_COUNT, MODEL_WIDTH, ADAPTER_RANK), MODEL_WIDTH ** -0.5, 0.0625, ((0, 64), (1, 8)))
    return dict(stored_inputs=stored_inputs, stored_output_gradient=stored_output_gradient, training_token_index=training_token_index, validation_inputs=validation_inputs, validation_output_gradient=validation_output_gradient, validation_row_skill=validation_row_skill, adapter_down_init=adapter_down_init)


def train_single_skill(inputs):
    stored_act, stored_cot, chosen, down_factor = inputs
    train_act = jnp.take(stored_act, chosen, axis=0)
    train_cot = jnp.take(stored_cot, chosen, axis=0)
    proj = jnp.dot(train_act, down_factor, preferred_element_type=jnp.float32).astype(jnp.bfloat16)
    product = lax.dot_general(proj, train_cot, (((0,), (0,)), ((), ())), preferred_element_type=jnp.float32)
    return (product * (-1.0 / TRAIN)).astype(jnp.bfloat16)


def reference(stored_inputs, stored_output_gradient, training_token_index, validation_inputs, validation_output_gradient, validation_row_skill, adapter_down_init):
    adapter_up_init = lax.map(train_single_skill, (stored_inputs, stored_output_gradient, training_token_index, adapter_down_init))

    def score_skill(skill_index):
        target_skills = (skill_index + jnp.arange(COLUMNS, dtype=jnp.int32) - REACH) % SKILL_COUNT
        selected_down = jnp.take(adapter_down_init, target_skills, axis=0).astype(jnp.float32)
        selected_up = jnp.take(adapter_up_init, target_skills, axis=0).astype(jnp.float32)
        valid_act = lax.dynamic_index_in_dim(validation_inputs, skill_index, 0, keepdims=False).astype(jnp.float32)
        valid_cot = lax.dynamic_index_in_dim(validation_output_gradient, skill_index, 0, keepdims=False).astype(jnp.float32)
        labels = lax.dynamic_index_in_dim(validation_row_skill, skill_index, 0, keepdims=False)
        own_mask = (labels == skill_index).astype(jnp.float32)
        other_mask = 1.0 - own_mask
        val_proj = jnp.einsum("vd,kdr->kvr", valid_act, selected_down, precision=lax.Precision.HIGHEST)
        cot_proj = jnp.einsum("vf,krf->kvr", valid_cot, selected_up, precision=lax.Precision.HIGHEST)
        row_change = jnp.sum(val_proj * cot_proj, axis=2)
        own_sum = jnp.sum(row_change * own_mask[None, :], axis=1)
        other_sum = jnp.sum(row_change * other_mask[None, :], axis=1)
        own_count = jnp.maximum(jnp.sum(own_mask), 1.0)
        other_count = jnp.maximum(jnp.sum(other_mask), 1.0)
        return own_sum / own_count, other_sum / other_count

    own_delta, other_delta = lax.map(score_skill, jnp.arange(SKILL_COUNT, dtype=jnp.int32))
    return own_delta, other_delta
```

```python
import functools

import jax
import jax.numpy as jnp
from jax import lax
from jax.experimental import pallas as pl
from jax.experimental.pallas import tpu as pltpu
from jax.sharding import PartitionSpec as P

F32 = jnp.float32
BF16 = jnp.bfloat16
STEPS = 4
CHIPS = 4
CORES = 2
GROUP = 8
NT = (((1,), (1,)), ((), ()))


def kernel(
    skills,
    reach,
    act_hbm,
    cot_hbm,
    index_ref,
    vact_hbm,
    vcot_hbm,
    label_ref,
    down_hbm,
    own_out,
    other_out,
    act,
    cot,
    vact,
    vcot,
    down_raw,
    down_own,
    down_all,
    up_own,
    up_all,
    part,
    part_in,
    share,
    full,
    send_f32,
    core_in,
    chip_out,
    chip_in,
    keep,
    own_f32,
    own_core_in,
    own_chip_out,
    own_chip_in,
    own_keep,
    table,
    table_in,
    load_sem,
    send_sem,
    recv_sem,
):
    me = lax.axis_index("skill")
    lane_pos = lax.axis_index("tensor")
    chip = lane_pos // CORES
    core = lax.rem(lane_pos, CORES)
    rank = down_own.shape[0]
    train = act.shape[0]
    piece = rank // CORES

    loads = []
    for n, (src, dst) in enumerate(
        [(down_hbm, down_raw), (act_hbm, act), (vact_hbm, vact), (cot_hbm, cot), (vcot_hbm, vcot)]
    ):
        copy = pltpu.make_async_copy(src, dst, load_sem.at[n])
        copy.start()
        loads.append(copy)
    load_down, load_act, load_vact, load_cot, load_vcot = loads

    def skill_at(shift):
        return (lax.rem(me + shift + skills, skills), lane_pos)

    def tensor_at(shift):
        return (me, lax.rem(lane_pos + shift, GROUP))

    def chip_at(shift):
        return (me, lax.rem(chip + shift, CHIPS) * CORES + core)

    sibling = (me, chip * CORES + (1 - core))

    barrier = pltpu.get_barrier_semaphore()
    partners = [skill_at(d) for d in (1, -1, reach, -reach)]
    partners += [tensor_at(d) for d in range(1, GROUP)]
    for partner in partners:
        pl.semaphore_signal(
            barrier, inc=1, device_id=partner, device_id_type=pl.DeviceIdType.MESH
        )

    started = []

    def send(src, dst, target):
        n = len(started)
        copy = pltpu.make_async_remote_copy(
            src_ref=src,
            dst_ref=dst,
            send_sem=send_sem.at[n],
            recv_sem=recv_sem.at[n],
            device_id=target,
            device_id_type=pl.DeviceIdType.MESH,
        )
        copy.start()
        started.append(copy)
        return copy

    def relay(own, held, step):
        def block(way):
            if step == 0:
                return own
            return held.at[step - 1, pl.ds(way * rank, rank)]

        def slot(way):
            return held.at[step, pl.ds(way * rank, rank)]

        return (
            send(block(0), slot(0), skill_at(1)),
            send(block(1), slot(1), skill_at(-1)),
            send(block(0), slot(2), skill_at(-reach)),
            send(block(1), slot(3), skill_at(reach)),
        )

    def near(copies):
        copies[0].wait_recv()
        copies[1].wait_recv()

    def far(copies):
        copies[2].wait_recv()
        copies[3].wait_recv()

    def scatter_cores(unit, product):
        rows = product.reshape(CHIPS, CORES, piece, product.shape[1])
        for c in range(CORES):
            send_f32[unit, c] = rows[:, c]
        return send(send_f32.at[unit, 1 - core], core_in.at[unit], sibling)

    def scatter_chips(unit, copy):
        copy.wait_recv()
        summed = send_f32[unit, core] + core_in[unit]
        chip_out[unit] = summed.astype(BF16)
        keep[unit] = summed
        return [
            send(
                chip_out.at[unit, lax.rem(chip + d, CHIPS)],
                chip_in.at[unit, d - 1],
                chip_at(d),
            )
            for d in range(1, CHIPS)
        ]

    def total(unit, copies):
        for copy in copies:
            copy.wait_recv()
        value = keep[unit, chip]
        for d in range(CHIPS - 1):
            value = value + chip_in[unit, d].astype(F32)
        return value

    load_down.wait()
    spot = lax.broadcasted_iota(jnp.int32, (rank, rank), 0)
    across = lax.broadcasted_iota(jnp.int32, (rank, rank), 1)
    eye = jnp.where(spot == across, 1.0, 0.0).astype(BF16)
    down_own[...] = lax.dot_general(
        eye, down_raw[...], NT, preferred_element_type=F32
    ).astype(BF16)
    pl.semaphore_wait(barrier, len(partners))
    down_moves = [relay(down_own, down_all, 0)]

    load_act.wait()
    part[...] = lax.dot_general(
        down_own[...], act[...], NT, preferred_element_type=F32
    ).reshape(part.shape)
    part_moves = [
        send(part.at[lax.rem(lane_pos + d, GROUP)], part_in.at[d - 1], tensor_at(d))
        for d in range(1, GROUP)
    ]
    load_vact.wait()
    own_val = lax.dot_general(down_own[...], vact[...], NT, preferred_element_type=F32)
    for copy in part_moves:
        copy.wait_recv()
    summed = part[lane_pos]
    for d in range(GROUP - 1):
        summed = summed + part_in[d]
    share[...] = summed
    full[lane_pos] = summed
    full_moves = [send(share, full.at[lane_pos], tensor_at(d)) for d in range(1, GROUP)]

    near(down_moves[0])
    down_moves.append(relay(down_own, down_all, 1))

    stored = lax.broadcasted_iota(jnp.int32, (train, train), 0)
    hits = jnp.where(stored == index_ref[...], 1.0, 0.0).astype(BF16)
    counts = lax.dot_general(
        jnp.ones((8, train), BF16), hits, NT, preferred_element_type=F32
    )[0:1]

    load_cot.wait()
    for copy in full_moves:
        copy.wait_recv()
    proj = full[...].reshape(rank, train).astype(BF16).astype(F32)
    weighted = proj * counts
    high = weighted.astype(BF16)
    low = (weighted - high.astype(F32)).astype(BF16)
    product = jnp.dot(
        jnp.concatenate([high, low], axis=0), cot[...], preferred_element_type=F32
    )
    up_own[...] = ((product[:rank] + product[rank:]) * (-1.0 / train)).astype(BF16)
    up_moves = [relay(up_own, up_all, 0)]

    def val_step(step):
        far(down_moves[step])
        return scatter_cores(
            step,
            lax.dot_general(down_all[step], vact[...], NT, preferred_element_type=F32),
        )

    def cot_step(step):
        far(up_moves[step])
        return scatter_cores(
            STEPS + step,
            lax.dot_general(up_all[step], vcot[...], NT, preferred_element_type=F32),
        )

    core_moves = {}
    chip_moves = {}
    core_moves[0] = val_step(0)
    near(down_moves[1])
    down_moves.append(relay(down_own, down_all, 2))

    load_vcot.wait()
    own_cot = lax.dot_general(up_own[...], vcot[...], NT, preferred_element_type=F32)
    for chip_n in range(CHIPS):
        for core_n in range(CORES):
            at = (chip_n * CORES + core_n) * (rank // GROUP)
            own_f32[core_n, chip_n, 0:8] = own_val[at : at + 8]
            own_f32[core_n, chip_n, 8:16] = own_cot[at : at + 8]
    own_core = send(own_f32.at[1 - core], own_core_in, sibling)
    chip_moves[0] = scatter_chips(0, core_moves[0])

    near(down_moves[2])
    down_moves.append(relay(down_own, down_all, 3))
    core_moves[1] = val_step(1)

    near(up_moves[0])
    up_moves.append(relay(up_own, up_all, 1))

    own_core.wait_recv()
    own_sum = own_f32[core] + own_core_in[...]
    own_chip_out[...] = own_sum.astype(BF16)
    own_keep[...] = own_sum
    own_chip = [
        send(own_chip_out.at[lax.rem(chip + d, CHIPS)], own_chip_in.at[d - 1], chip_at(d))
        for d in range(1, CHIPS)
    ]
    chip_moves[1] = scatter_chips(1, core_moves[1])
    core_moves[4] = cot_step(0)
    core_moves[2] = val_step(2)
    chip_moves[4] = scatter_chips(4, core_moves[4])
    chip_moves[2] = scatter_chips(2, core_moves[2])

    near(up_moves[1])
    up_moves.append(relay(up_own, up_all, 2))
    near(down_moves[3])
    core_moves[3] = val_step(3)
    core_moves[5] = cot_step(1)
    chip_moves[3] = scatter_chips(3, core_moves[3])
    chip_moves[5] = scatter_chips(5, core_moves[5])

    near(up_moves[2])
    up_moves.append(relay(up_own, up_all, 3))
    core_moves[6] = cot_step(2)
    chip_moves[6] = scatter_chips(6, core_moves[6])

    def change(step):
        value = total(step, chip_moves[step]) * total(
            STEPS + step, chip_moves[STEPS + step]
        )
        return jnp.sum(value, axis=0, keepdims=True)

    for copy in own_chip:
        copy.wait_recv()
    own_piece = own_keep[chip]
    for d in range(CHIPS - 1):
        own_piece = own_piece + own_chip_in[d].astype(F32)
    changes = [change(0), change(1)]
    own_change = jnp.sum(own_piece[0:8] * own_piece[8:16], axis=0, keepdims=True)

    near(up_moves[3])
    core_moves[7] = cot_step(3)
    chip_moves[7] = scatter_chips(7, core_moves[7])
    changes.append(change(2))
    changes.append(change(3))

    own_mask = (label_ref[...] == me).astype(F32)
    other_mask = 1.0 - own_mask
    stack = jnp.concatenate(
        changes + [own_change, jnp.zeros((3, own_change.shape[1]), F32)], axis=0
    )
    own_part = jnp.sum(stack * own_mask, axis=1, keepdims=True)
    other_part = jnp.sum(stack * other_mask, axis=1, keepdims=True)

    row = lax.broadcasted_iota(jnp.int32, (8, 128), 0)
    column = lax.broadcasted_iota(jnp.int32, (8, 128), 1)
    from_behind = chip == 0
    from_ahead = chip == 1
    from_far_ahead = chip == 2
    place = jnp.where(
        from_behind,
        reach - 1 - row,
        jnp.where(
            from_ahead, reach + 1 + row, jnp.where(from_far_ahead, 2 * reach - row, row)
        ),
    )
    place = jnp.where(row == STEPS, reach, place)
    chosen = (place == column) & (row <= STEPS)
    own_row = jnp.sum(jnp.where(chosen, own_part, 0.0), axis=0, keepdims=True)
    other_row = jnp.sum(jnp.where(chosen, other_part, 0.0), axis=0, keepdims=True)
    table[...] = jnp.where(row == 0, own_row, jnp.where(row == 1, other_row, 0.0))
    table_moves = [send(table, table_in.at[d - 1], tensor_at(d)) for d in range(1, GROUP)]
    own_count = jnp.maximum(jnp.sum(own_mask, axis=1, keepdims=True), 1.0)
    other_count = jnp.maximum(jnp.sum(other_mask, axis=1, keepdims=True), 1.0)
    for copy in table_moves:
        copy.wait_recv()
    result = jnp.zeros((8, 128), F32)
    for t in range(GROUP):
        away = lax.rem(lane_pos - t + GROUP, GROUP)
        theirs = table_in[lax.max(away - 1, 0)]
        result = result + jnp.where(away == 0, table[...], theirs)
    columns = own_out.shape[1]
    own_out[...] = result[0:1, :columns] / own_count
    other_out[...] = result[1:2, :columns] / other_count
    for copy in started:
        copy.wait_send()


def on_device(
    stored_inputs,
    stored_output_gradient,
    training_token_index,
    validation_inputs,
    validation_output_gradient,
    validation_row_skill,
    adapter_down_init,
):
    skills = lax.axis_size("skill")
    reach = skills // 8
    columns = 2 * reach + 1
    _, train, width = stored_inputs.shape
    hidden = stored_output_gradient.shape[2]
    rows = validation_inputs.shape[1]
    rank = adapter_down_init.shape[2]
    piece = rank // CORES
    units = 2 * STEPS
    copies = 2 * 4 * STEPS + 3 * (GROUP - 1) + units * CHIPS + CHIPS
    any_spec = pl.BlockSpec(memory_space=pl.ANY)
    vmem_spec = pl.BlockSpec(memory_space=pltpu.VMEM)
    return pl.pallas_call(
        functools.partial(kernel, skills, reach),
        out_shape=(
            jax.ShapeDtypeStruct((1, columns), F32),
            jax.ShapeDtypeStruct((1, columns), F32),
        ),
        in_specs=[any_spec, any_spec, vmem_spec, any_spec, any_spec, vmem_spec, any_spec],
        out_specs=(vmem_spec, vmem_spec),
        scratch_shapes=[
            pltpu.VMEM((train, width), BF16),
            pltpu.VMEM((train, hidden), BF16),
            pltpu.VMEM((rows, width), BF16),
            pltpu.VMEM((rows, hidden), BF16),
            pltpu.VMEM((width, rank), BF16),
            pltpu.VMEM((rank, width), BF16),
            pltpu.VMEM((STEPS, 4 * rank, width), BF16),
            pltpu.VMEM((rank, hidden), BF16),
            pltpu.VMEM((STEPS, 4 * rank, hidden), BF16),
            pltpu.VMEM((GROUP, rank // GROUP, train), F32),
            pltpu.VMEM((GROUP - 1, rank // GROUP, train), F32),
            pltpu.VMEM((rank // GROUP, train), F32),
            pltpu.VMEM((GROUP, rank // GROUP, train), F32),
            pltpu.VMEM((units, CORES, CHIPS, piece, rows), F32),
            pltpu.VMEM((units, CHIPS, piece, rows), F32),
            pltpu.VMEM((units, CHIPS, piece, rows), BF16),
            pltpu.VMEM((units, CHIPS - 1, piece, rows), BF16),
            pltpu.VMEM((units, CHIPS, piece, rows), F32),
            pltpu.VMEM((CORES, CHIPS, 16, rows), F32),
            pltpu.VMEM((CHIPS, 16, rows), F32),
            pltpu.VMEM((CHIPS, 16, rows), BF16),
            pltpu.VMEM((CHIPS - 1, 16, rows), BF16),
            pltpu.VMEM((CHIPS, 16, rows), F32),
            pltpu.VMEM((8, 128), F32),
            pltpu.VMEM((GROUP - 1, 8, 128), F32),
            pltpu.SemaphoreType.DMA((5,)),
            pltpu.SemaphoreType.DMA((copies,)),
            pltpu.SemaphoreType.DMA((copies,)),
        ],
        compiler_params=pltpu.CompilerParams(
            collective_id=0, has_side_effects=True, vmem_limit_bytes=48 * 1024 * 1024
        ),
    )(
        stored_inputs[0],
        stored_output_gradient[0],
        training_token_index,
        validation_inputs[0],
        validation_output_gradient[0],
        validation_row_skill,
        adapter_down_init[0],
    )


def solution(mesh):
    in_specs = (
        P("skill", None, "tensor"),
        P("skill", None, "tensor"),
        P("skill", None),
        P("skill", None, "tensor"),
        P("skill", None, "tensor"),
        P("skill", None),
        P("skill", "tensor", None),
    )
    out_specs = (P("skill", None), P("skill", None))
    return jax.shard_map(
        on_device, mesh=mesh, in_specs=in_specs, out_specs=out_specs, check_vma=False
    )
```

```python
import functools

import jax
import jax.numpy as jnp
from jax import lax
from jax.experimental import pallas as pl
from jax.experimental.pallas import tpu as pltpu
from jax.sharding import PartitionSpec as P

F32 = jnp.float32
BF16 = jnp.bfloat16
STEPS = 4
BLOCKS = 16
CHIPS = 4
CORES = 2
GROUP = 8
NT = (((1,), (1,)), ((), ()))


def kernel(
    skills,
    reach,
    act_hbm,
    cot_hbm,
    index_ref,
    vact_hbm,
    vcot_hbm,
    label_ref,
    down_hbm,
    own_out,
    other_out,
    act,
    cot,
    vact,
    vcot,
    down_own,
    down_all,
    up_own,
    up_all,
    tail_own,
    tail_all,
    part,
    part_in,
    share,
    full,
    send_f32,
    core_in,
    chip_out,
    chip_in,
    keep,
    own_f32,
    own_core_in,
    own_chip_out,
    own_chip_in,
    own_keep,
    table,
    table_in,
    load_sem,
    send_sem,
    recv_sem,
    block_sem,
):
    me = lax.axis_index("skill")
    lane_pos = lax.axis_index("tensor")
    chip = lane_pos // CORES
    core = lax.rem(lane_pos, CORES)
    rank = down_own.shape[0]
    train = act.shape[0]
    piece = rank // CORES

    loads = []
    for n, (src, dst) in enumerate(
        [(down_hbm, down_own), (act_hbm, act), (vact_hbm, vact), (cot_hbm, cot), (vcot_hbm, vcot)]
    ):
        copy = pltpu.make_async_copy(src, dst, load_sem.at[n])
        copy.start()
        loads.append(copy)
    load_down, load_act, load_vact, load_cot, load_vcot = loads

    def skill_at(shift):
        return (lax.rem(me + shift + skills, skills), lane_pos)

    def tensor_at(shift):
        return (me, lax.rem(lane_pos + shift, GROUP))

    def chip_at(shift):
        return (me, lax.rem(chip + shift, CHIPS) * CORES + core)

    sibling = (me, chip * CORES + (1 - core))

    barrier = pltpu.get_barrier_semaphore()
    depth = lax.rem(me, reach)
    low_half = depth < reach // 2

    def ring_at(shift):
        return (me - depth + lax.rem(depth + shift + reach, reach), lane_pos)

    partners = [ring_at(1), ring_at(-1), skill_at(reach), skill_at(-reach)]
    partners += [tensor_at(d) for d in range(1, GROUP)]
    for partner in partners:
        pl.semaphore_signal(
            barrier, inc=1, device_id=partner, device_id_type=pl.DeviceIdType.MESH
        )

    started = []
    started_if = []

    def send(src, dst, target):
        n = len(started) + len(started_if)
        copy = pltpu.make_async_remote_copy(
            src_ref=src,
            dst_ref=dst,
            send_sem=send_sem.at[n],
            recv_sem=recv_sem.at[n],
            device_id=target,
            device_id_type=pl.DeviceIdType.MESH,
        )
        copy.start()
        started.append(copy)
        return copy

    class Stream:
        def __init__(self, own, held):
            self.own, self.held = own, held
            self.base = len(streams) * BLOCKS
            streams.append(self)

        def block(self, slot):
            return self.own if slot is None else self.held.at[slot]

        def send(self, source, slot, target, when=None):
            n = len(started) + len(started_if)
            copy = pltpu.make_async_remote_copy(
                src_ref=self.block(source),
                dst_ref=self.held.at[slot],
                send_sem=send_sem.at[n],
                recv_sem=block_sem.at[self.base + slot],
                device_id=target,
                device_id_type=pl.DeviceIdType.MESH,
            )
            if when is None:
                copy.start()
                started.append(copy)
            else:
                pl.when(when)(copy.start)
                started_if.append((when, copy))

        def wait(self, *slots):
            for slot in slots:
                pltpu.make_async_remote_copy(
                    src_ref=self.own,
                    dst_ref=self.held.at[slot],
                    send_sem=send_sem.at[0],
                    recv_sem=block_sem.at[self.base + slot],
                    device_id=sibling,
                    device_id_type=pl.DeviceIdType.MESH,
                ).wait_recv()

        def step0(self):
            self.send(None, 0, ring_at(1))
            self.send(None, 1, ring_at(-1))
            self.send(None, 2, skill_at(-reach))
            self.send(None, 3, skill_at(reach))

        def step1(self):
            self.wait(0, 1)
            self.send(0, 4, ring_at(1))
            self.send(1, 5, ring_at(-1))
            self.send(0, 6, skill_at(-reach), depth >= 1)
            self.send(1, 7, skill_at(reach), depth <= reach - 2)

        def wrap1(self):
            self.wait(2, 3)
            self.send(3, 6, ring_at(1), depth == reach - 1)
            self.send(2, 7, ring_at(-1), depth == 0)

        def step2(self):
            self.wait(4, 5)
            self.send(4, 8, ring_at(1))
            self.send(5, 9, ring_at(-1))
            self.send(4, jnp.where(low_half, 13, 10), skill_at(-reach), depth >= 2)
            self.send(5, jnp.where(low_half, 10, 13), skill_at(reach), depth <= reach - 3)

        def wrap2(self):
            self.wait(6, 7)
            self.send(6, 13, ring_at(1), depth == 0)
            self.send(7, 13, ring_at(-1), depth == reach - 1)

        def step3(self, ahead):
            self.wait(8, 9)
            if ahead:
                self.send(8, 12, ring_at(1))
            else:
                self.send(9, 12, ring_at(-1))
            self.send(8, jnp.where(low_half, 14, 11), skill_at(-reach), depth >= 3)
            self.send(9, jnp.where(low_half, 11, 14), skill_at(reach), depth <= reach - 4)

        def step4(self):
            self.wait(12)
            self.send(12, 15, skill_at(jnp.where(low_half, reach, -reach)))

        def relay1(self):
            self.wait(15)
            self.send(
                15,
                14,
                ring_at(jnp.where(low_half, -1, 1)),
                (depth != 0) & (depth != reach - 1),
            )

        def relay2(self):
            self.wait(14)
            self.send(
                14,
                13,
                ring_at(jnp.where(low_half, -1, 1)),
                (depth == 1) | (depth == reach - 2),
            )

    streams = []

    def scatter_cores(unit, product):
        rows = product.reshape(CHIPS, CORES, piece, product.shape[1])
        for c in range(CORES):
            send_f32[unit, c] = rows[:, c]
        return send(send_f32.at[unit, 1 - core], core_in.at[unit], sibling)

    def scatter_chips(unit, copy):
        copy.wait_recv()
        summed = send_f32[unit, core] + core_in[unit]
        chip_out[unit] = summed.astype(BF16)
        keep[unit] = summed
        return [
            send(
                chip_out.at[unit, lax.rem(chip + d, CHIPS)],
                chip_in.at[unit, d - 1],
                chip_at(d),
            )
            for d in range(1, CHIPS)
        ]

    def total(unit, copies):
        for copy in copies:
            copy.wait_recv()
        value = keep[unit, chip]
        for d in range(CHIPS - 1):
            value = value + chip_in[unit, d].astype(F32)
        return value

    load_down.wait()
    pl.semaphore_wait(barrier, len(partners))
    down = Stream(down_own, down_all)
    up = Stream(up_own, up_all)
    tail = Stream(tail_own, tail_all)
    split = up_own.shape[1]
    down.step0()

    load_act.wait()
    part[...] = lax.dot_general(
        down_own[...], act[...], NT, preferred_element_type=F32
    ).reshape(part.shape)
    part_moves = [
        send(part.at[lax.rem(lane_pos + d, GROUP)], part_in.at[d - 1], tensor_at(d))
        for d in range(1, GROUP)
    ]
    load_vact.wait()
    own_val = lax.dot_general(down_own[...], vact[...], NT, preferred_element_type=F32)
    for copy in part_moves:
        copy.wait_recv()
    summed = part[lane_pos]
    for d in range(GROUP - 1):
        summed = summed + part_in[d]
    share[...] = summed
    full[lane_pos] = summed
    full_moves = [send(share, full.at[lane_pos], tensor_at(d)) for d in range(1, GROUP)]

    down.step1()
    down.wrap1()

    stored = lax.broadcasted_iota(jnp.int32, (train, train), 0)
    hits = jnp.where(stored == index_ref[...], 1.0, 0.0).astype(BF16)
    counts = lax.dot_general(
        jnp.ones((8, train), BF16), hits, NT, preferred_element_type=F32
    )[0:1]

    load_cot.wait()
    for copy in full_moves:
        copy.wait_recv()
    proj = full[...].reshape(rank, train).astype(BF16).astype(F32)
    weighted = proj * counts
    high = weighted.astype(BF16)
    low = (weighted - high.astype(F32)).astype(BF16)
    product = jnp.dot(
        jnp.concatenate([high, low], axis=0), cot[...], preferred_element_type=F32
    )
    factor = ((product[:rank] + product[rank:]) * (-1.0 / train)).astype(BF16)
    up_own[...] = factor[:, :split]
    up.step0()
    tail_own[...] = factor[:, split:]
    tail.step0()
    down.step2()

    def val_step(unit):
        rows = down_all[4 * unit : 4 * unit + 4].reshape(4 * rank, down_own.shape[1])
        return scatter_cores(
            unit, lax.dot_general(rows, vact[...], NT, preferred_element_type=F32)
        )

    def cot_dot(first, second):
        return lax.dot_general(
            first, vcot[:, :split], NT, preferred_element_type=F32
        ) + lax.dot_general(second, vcot[:, split:], NT, preferred_element_type=F32)

    def cot_step(unit):
        rows = up_all[4 * unit : 4 * unit + 4].reshape(4 * rank, split)
        rest = tail_all[4 * unit : 4 * unit + 4].reshape(4 * rank, tail_own.shape[1])
        return scatter_cores(STEPS + unit, cot_dot(rows, rest))

    core_moves = {}
    chip_moves = {}
    core_moves[0] = val_step(0)
    down.wrap2()
    up.step1()
    tail.step1()

    load_vcot.wait()
    own_cot = cot_dot(up_own[...], tail_own[...])
    for chip_n in range(CHIPS):
        for core_n in range(CORES):
            at = (chip_n * CORES + core_n) * (rank // GROUP)
            own_f32[core_n, chip_n, 0:8] = own_val[at : at + 8]
            own_f32[core_n, chip_n, 8:16] = own_cot[at : at + 8]
    own_core = send(own_f32.at[1 - core], own_core_in, sibling)
    chip_moves[0] = scatter_chips(0, core_moves[0])

    down.step3(True)
    up.wrap1()
    tail.wrap1()
    core_moves[1] = val_step(1)
    down.step4()
    up.step2()
    tail.step2()

    own_core.wait_recv()
    own_sum = own_f32[core] + own_core_in[...]
    own_chip_out[...] = own_sum.astype(BF16)
    own_keep[...] = own_sum
    own_chip = [
        send(own_chip_out.at[lax.rem(chip + d, CHIPS)], own_chip_in.at[d - 1], chip_at(d))
        for d in range(1, CHIPS)
    ]
    chip_moves[1] = scatter_chips(1, core_moves[1])
    core_moves[4] = cot_step(0)
    down.relay1()
    up.wrap2()
    tail.wrap2()
    chip_moves[4] = scatter_chips(4, core_moves[4])
    up.step3(False)
    tail.step3(True)
    core_moves[5] = cot_step(1)
    down.wait(10, 11)
    core_moves[2] = val_step(2)
    down.relay2()
    up.step4()
    tail.step4()
    chip_moves[5] = scatter_chips(5, core_moves[5])
    chip_moves[2] = scatter_chips(2, core_moves[2])
    down.wait(13)
    core_moves[3] = val_step(3)
    up.wait(10, 11)
    tail.wait(10, 11)
    core_moves[6] = cot_step(2)
    up.relay1()
    tail.relay1()
    chip_moves[3] = scatter_chips(3, core_moves[3])
    chip_moves[6] = scatter_chips(6, core_moves[6])

    def change(step):
        value = total(step, chip_moves[step]) * total(
            STEPS + step, chip_moves[STEPS + step]
        )
        return jnp.sum(value, axis=0, keepdims=True)

    for copy in own_chip:
        copy.wait_recv()
    own_piece = own_keep[chip]
    for d in range(CHIPS - 1):
        own_piece = own_piece + own_chip_in[d].astype(F32)
    changes = [change(0), change(1)]
    own_change = jnp.sum(own_piece[0:8] * own_piece[8:16], axis=0, keepdims=True)

    up.relay2()
    tail.relay2()
    up.wait(13)
    tail.wait(13)
    core_moves[7] = cot_step(3)
    chip_moves[7] = scatter_chips(7, core_moves[7])
    changes.append(change(2))
    changes.append(change(3))

    own_mask = (label_ref[...] == me).astype(F32)
    other_mask = 1.0 - own_mask
    stack = jnp.concatenate(
        changes + [own_change, jnp.zeros((3, own_change.shape[1]), F32)], axis=0
    )
    own_part = jnp.sum(stack * own_mask, axis=1, keepdims=True)
    other_part = jnp.sum(stack * other_mask, axis=1, keepdims=True)

    row = lax.broadcasted_iota(jnp.int32, (8, 128), 0)
    column = lax.broadcasted_iota(jnp.int32, (8, 128), 1)
    def ring_column(d):
        return jnp.where(depth >= d, reach - d, 2 * reach - d)

    def far_column(p):
        return jnp.where(depth >= p, 2 * reach - p, reach - p)

    def pick(p, q):
        return jnp.where(low_half, far_column(p), far_column(q))

    held_columns = (
        (ring_column(1), ring_column(7), far_column(0), far_column(8)),
        (ring_column(2), ring_column(6), far_column(1), far_column(7)),
        (ring_column(3), ring_column(5), pick(6, 2), pick(5, 3)),
        (ring_column(4), pick(2, 6), pick(3, 5), far_column(4)),
    )
    place = jnp.full((8, 128), reach, jnp.int32)
    for unit in range(STEPS):
        first, second, third, fourth = held_columns[unit]
        mine = jnp.where(
            chip == 0,
            first,
            jnp.where(chip == 1, second, jnp.where(chip == 2, third, fourth)),
        )
        place = jnp.where(row == unit, mine, place)
    chosen = (place == column) & (row <= STEPS)
    own_row = jnp.sum(jnp.where(chosen, own_part, 0.0), axis=0, keepdims=True)
    other_row = jnp.sum(jnp.where(chosen, other_part, 0.0), axis=0, keepdims=True)
    table[...] = jnp.where(row == 0, own_row, jnp.where(row == 1, other_row, 0.0))
    table_moves = [send(table, table_in.at[d - 1], tensor_at(d)) for d in range(1, GROUP)]
    own_count = jnp.maximum(jnp.sum(own_mask, axis=1, keepdims=True), 1.0)
    other_count = jnp.maximum(jnp.sum(other_mask, axis=1, keepdims=True), 1.0)
    for copy in table_moves:
        copy.wait_recv()
    result = jnp.zeros((8, 128), F32)
    for t in range(GROUP):
        away = lax.rem(lane_pos - t + GROUP, GROUP)
        theirs = table_in[lax.max(away - 1, 0)]
        result = result + jnp.where(away == 0, table[...], theirs)
    columns = own_out.shape[1]
    own_out[...] = result[0:1, :columns] / own_count
    other_out[...] = result[1:2, :columns] / other_count
    for copy in started:
        copy.wait_send()
    for when, copy in started_if:
        pl.when(when)(copy.wait_send)


def on_device(
    stored_inputs,
    stored_output_gradient,
    training_token_index,
    validation_inputs,
    validation_output_gradient,
    validation_row_skill,
    adapter_down_init,
):
    skills = lax.axis_size("skill")
    reach = skills // 8
    columns = 2 * reach + 1
    _, train, width = stored_inputs.shape
    hidden = stored_output_gradient.shape[2]
    rows = validation_inputs.shape[1]
    rank = adapter_down_init.shape[2]
    piece = rank // CORES
    split = (hidden // 256 + 1) * 128
    units = 2 * STEPS
    copies = 3 * 22 + 3 * (GROUP - 1) + units * CHIPS + CHIPS
    any_spec = pl.BlockSpec(memory_space=pl.ANY)
    vmem_spec = pl.BlockSpec(memory_space=pltpu.VMEM)
    return pl.pallas_call(
        functools.partial(kernel, skills, reach),
        out_shape=(
            jax.ShapeDtypeStruct((1, columns), F32),
            jax.ShapeDtypeStruct((1, columns), F32),
        ),
        in_specs=[any_spec, any_spec, vmem_spec, any_spec, any_spec, vmem_spec, any_spec],
        out_specs=(vmem_spec, vmem_spec),
        scratch_shapes=[
            pltpu.VMEM((train, width), BF16),
            pltpu.VMEM((train, hidden), BF16),
            pltpu.VMEM((rows, width), BF16),
            pltpu.VMEM((rows, hidden), BF16),
            pltpu.VMEM((rank, width), BF16),
            pltpu.VMEM((BLOCKS, rank, width), BF16),
            pltpu.VMEM((rank, split), BF16),
            pltpu.VMEM((BLOCKS, rank, split), BF16),
            pltpu.VMEM((rank, hidden - split), BF16),
            pltpu.VMEM((BLOCKS, rank, hidden - split), BF16),
            pltpu.VMEM((GROUP, rank // GROUP, train), F32),
            pltpu.VMEM((GROUP - 1, rank // GROUP, train), F32),
            pltpu.VMEM((rank // GROUP, train), F32),
            pltpu.VMEM((GROUP, rank // GROUP, train), F32),
            pltpu.VMEM((units, CORES, CHIPS, piece, rows), F32),
            pltpu.VMEM((units, CHIPS, piece, rows), F32),
            pltpu.VMEM((units, CHIPS, piece, rows), BF16),
            pltpu.VMEM((units, CHIPS - 1, piece, rows), BF16),
            pltpu.VMEM((units, CHIPS, piece, rows), F32),
            pltpu.VMEM((CORES, CHIPS, 16, rows), F32),
            pltpu.VMEM((CHIPS, 16, rows), F32),
            pltpu.VMEM((CHIPS, 16, rows), BF16),
            pltpu.VMEM((CHIPS - 1, 16, rows), BF16),
            pltpu.VMEM((CHIPS, 16, rows), F32),
            pltpu.VMEM((8, 128), F32),
            pltpu.VMEM((GROUP - 1, 8, 128), F32),
            pltpu.SemaphoreType.DMA((5,)),
            pltpu.SemaphoreType.DMA((copies,)),
            pltpu.SemaphoreType.DMA((copies,)),
            pltpu.SemaphoreType.DMA((3 * BLOCKS,)),
        ],
        compiler_params=pltpu.CompilerParams(
            collective_id=0, has_side_effects=True, vmem_limit_bytes=60 * 1024 * 1024
        ),
    )(
        stored_inputs[0],
        stored_output_gradient[0],
        training_token_index,
        validation_inputs[0],
        validation_output_gradient[0],
        validation_row_skill,
        jnp.swapaxes(adapter_down_init[0], 0, 1),
    )


def solution(mesh):
    in_specs = (
        P("skill", None, "tensor"),
        P("skill", None, "tensor"),
        P("skill", None),
        P("skill", None, "tensor"),
        P("skill", None, "tensor"),
        P("skill", None),
        P("skill", "tensor", None),
    )
    out_specs = (P("skill", None), P("skill", None))
    return jax.shard_map(
        on_device, mesh=mesh, in_specs=in_specs, out_specs=out_specs, check_vma=False
    )
```

```python
import functools

import jax
import jax.numpy as jnp
from jax import lax
from jax.experimental import pallas as pl
from jax.experimental.pallas import tpu as pltpu
from jax.sharding import PartitionSpec as P

F32 = jnp.float32
BF16 = jnp.bfloat16
STEPS = 4
BLOCKS = 17
PIECES = 2
CHIPS = 4
CORES = 2
GROUP = 8
LINE = 4
PASSING = 16
NT = (((1,), (1,)), ((), ()))


def kernel(
    skills,
    reach,
    act_hbm,
    cot_hbm,
    index_ref,
    vact_hbm,
    vcot_hbm,
    label_ref,
    down_hbm,
    own_out,
    other_out,
    act,
    cot,
    vact,
    vcot,
    down_own,
    down_all,
    up_own0,
    up_all0,
    up_own1,
    up_all1,
    part,
    part_in,
    share,
    full,
    unit_halves,
    unit_core_in,
    unit_out,
    unit_chip_in,
    unit_full,
    own_halves,
    own_core_in,
    own_out_f32,
    own_chip_in,
    own_full,
    table,
    table_in,
    load_sem,
    send_sem,
    recv_sem,
    block_sem,
):
    unit_refs = (unit_halves, unit_core_in, unit_out, unit_chip_in, unit_full)
    own_refs = (own_halves, own_core_in, own_out_f32, own_chip_in, own_full)
    me = lax.axis_index("skill")
    lane_pos = lax.axis_index("tensor")
    chip = lane_pos // CORES
    core = lax.rem(lane_pos, CORES)
    rank = down_own.shape[0]
    train = act.shape[0]
    piece = rank // CORES

    loads = []
    for n, (src, dst) in enumerate(
        [(down_hbm, down_own), (act_hbm, act), (vact_hbm, vact), (cot_hbm, cot), (vcot_hbm, vcot)]
    ):
        copy = pltpu.make_async_copy(src, dst, load_sem.at[n])
        copy.start()
        loads.append(copy)
    load_down, load_act, load_vact, load_cot, load_vcot = loads

    def skill_at(shift):
        return (lax.rem(me + shift + skills, skills), lane_pos)

    def tensor_at(shift):
        return (me, lax.rem(lane_pos + shift, GROUP))

    def chip_at(shift):
        return (me, lax.rem(chip + shift, CHIPS) * CORES + core)

    sibling = (me, chip * CORES + (1 - core))

    barrier = pltpu.get_barrier_semaphore()
    depth = lax.rem(me, reach)
    half = reach // 2
    low_half = depth < half
    line = lax.rem(me // reach, LINE)
    first_in_line = line == 0
    last_in_line = line == LINE - 1

    def ring_at(shift):
        return (me - depth + lax.rem(depth + shift + reach, reach), lane_pos)

    partners = [ring_at(1), ring_at(-1), skill_at(reach), skill_at(-reach)]
    partners += [tensor_at(d) for d in range(1, GROUP)]
    for partner in partners:
        pl.semaphore_signal(
            barrier, inc=1, device_id=partner, device_id_type=pl.DeviceIdType.MESH
        )

    started = []
    started_if = []

    def send(src, dst, target):
        n = len(started) + len(started_if)
        copy = pltpu.make_async_remote_copy(
            src_ref=src,
            dst_ref=dst,
            send_sem=send_sem.at[n],
            recv_sem=recv_sem.at[n],
            device_id=target,
            device_id_type=pl.DeviceIdType.MESH,
        )
        copy.start()
        started.append(copy)
        return copy

    class Stream:
        def __init__(self, own, held):
            self.own, self.held = own, held
            self.base = len(streams) * BLOCKS
            streams.append(self)

        def block(self, slot):
            return self.own if slot is None else self.held.at[slot]

        def send(self, source, slot, target, when=None):
            n = len(started) + len(started_if)
            copy = pltpu.make_async_remote_copy(
                src_ref=self.block(source),
                dst_ref=self.held.at[slot],
                send_sem=send_sem.at[n],
                recv_sem=block_sem.at[self.base + slot],
                device_id=target,
                device_id_type=pl.DeviceIdType.MESH,
            )
            if when is None:
                copy.start()
                started.append(copy)
            else:
                pl.when(when)(copy.start)
                started_if.append((when, copy))

        def wait(self, *slots):
            for slot in slots:
                pltpu.make_async_remote_copy(
                    src_ref=self.own,
                    dst_ref=self.held.at[slot],
                    send_sem=send_sem.at[0],
                    recv_sem=block_sem.at[self.base + slot],
                    device_id=sibling,
                    device_id_type=pl.DeviceIdType.MESH,
                ).wait_recv()

        def step0(self):
            self.send(None, 0, ring_at(1))
            self.send(None, 1, ring_at(-1))
            self.send(None, 2, skill_at(-reach))
            self.send(None, 3, skill_at(reach))

        def step1(self):
            self.wait(0, 1)
            self.send(0, 4, ring_at(1))
            self.send(1, 5, ring_at(-1))
            self.send(0, 6, skill_at(-reach), depth >= 1)
            self.send(1, 7, skill_at(reach), depth <= reach - 2)

        def step2(self):
            self.wait(4, 5)
            self.send(4, 8, ring_at(1))
            self.send(5, 9, ring_at(-1))
            self.send(
                4, 10, skill_at(jnp.where(depth >= 2, -reach, reach)), (depth >= 2) | ~last_in_line
            )
            self.send(
                5, 11, skill_at(jnp.where(depth <= reach - 3, reach, -reach)), (depth <= reach - 3) | ~first_in_line
            )

        def wrap(self):
            self.wait(2, 3)
            self.send(3, 6, ring_at(1), depth == reach - 1)
            self.send(2, 7, ring_at(-1), depth == 0)
            self.send(
                jnp.where(low_half, 2, 3),
                PASSING,
                ring_at(jnp.where(low_half, -1, 1)),
                (first_in_line & (depth == reach - 2)) | (last_in_line & (depth == 1)),
            )

        def wrap2(self):
            passing = (first_in_line & (depth == reach - 1)) | (last_in_line & (depth == 0))
            pl.when(passing)(lambda: self.wait(PASSING))
            self.send(
                PASSING,
                jnp.where(low_half, 11, 10),
                ring_at(jnp.where(low_half, -1, 1)),
                passing,
            )
            self.wait(6, 7)
            self.send(
                jnp.where(low_half, 6, 7),
                jnp.where(low_half, 10, 11),
                ring_at(jnp.where(low_half, 1, -1)),
                (first_in_line & (depth == 0)) | (last_in_line & (depth == reach - 1)),
            )
        def relay2(self):
            self.wait(10, 11)
            self.send(11, 14, ring_at(-1), (depth >= 1) & (depth <= half))
            self.send(10, 13, ring_at(1), (depth >= half - 1) & (depth <= reach - 2))

        def step3(self):
            self.wait(8, 9)
            self.send(8, 12, ring_at(1), lax.rem(depth + 1, reach) < half)
            self.send(9, 12, ring_at(-1), lax.rem(depth + reach - 1, reach) >= half)
            self.send(
                8,
                13,
                skill_at(jnp.where(depth == half - 1, -reach, reach)),
                low_half,
            )
            self.send(
                9,
                14,
                skill_at(jnp.where(depth == half, reach, -reach)),
                ~low_half,
            )

        def relay3(self):
            near_slot = jnp.where(low_half, 14, 13)
            self.wait(near_slot)
            self.send(
                near_slot,
                15,
                ring_at(jnp.where(low_half, -1, 1)),
                (depth >= 1) & (depth <= reach - 2),
            )
            middle = (depth == half) | (depth == half - 1)
            pl.when(middle)(lambda: self.wait(jnp.where(low_half, 13, 14)))
            self.send(
                jnp.where(low_half, 13, 14), 15, ring_at(jnp.where(low_half, 1, -1)), middle
            )

        def last(self):
            self.wait(12, 15)
            pl.when((depth < half - 1) | (depth > half))(
                lambda: self.wait(jnp.where(low_half, 13, 14))
            )

    streams = []

    class Projection:
        def __init__(self, refs, index):
            self.halves, self.core_in, self.out, self.chip_in, self.full = [
                ref.at[index] for ref in refs
            ]

        def to_core(self, product):
            parts = product.reshape(CHIPS, CORES, -1, product.shape[1])
            for c in range(CORES):
                self.halves[c] = parts[:, c]
            self.move = send(self.halves.at[1 - core], self.core_in, sibling)

        def to_owners(self):
            self.move.wait_recv()
            both = self.halves[core] + self.core_in[...]
            self.out[...] = both.astype(self.out.dtype)
            self.core_in[...] = both
            self.moves = [
                send(
                    self.out.at[lax.rem(chip + d, CHIPS)], self.chip_in.at[d - 1], chip_at(d)
                )
                for d in range(1, CHIPS)
            ]

        def to_chips(self):
            value = self.core_in[chip]
            for d in range(CHIPS - 1):
                self.moves[d].wait_recv()
                value = value + self.chip_in[d].astype(F32)
            mine = self.full.at[core, chip]
            mine[...] = value.astype(self.full.dtype)
            self.moves = [send(mine, mine, chip_at(d)) for d in range(1, CHIPS)]

        def to_sibling(self):
            for move in self.moves:
                move.wait_recv()
            self.move = send(self.full.at[core], self.full.at[core], sibling)

        def change(self, product):
            self.move.wait_recv()
            parts = product.reshape(CHIPS, CORES, -1, product.shape[1])
            sums = []
            for c in range(CORES):
                sums.append(jnp.sum(parts[:, c] * self.full[c].astype(F32), axis=1))
            return sums[0] + sums[1]

    load_down.wait()
    load_act.wait()
    part[...] = lax.dot_general(
        down_own[...], act[...], NT, preferred_element_type=F32
    ).reshape(part.shape)
    pl.semaphore_wait(barrier, len(partners))
    down = Stream(down_own, down_all)
    ups = [Stream(*refs) for refs in ((up_own0, up_all0), (up_own1, up_all1))]
    edges = [0]
    for up in ups:
        edges.append(edges[-1] + up.own.shape[1])
    down.step0()

    part_moves = [
        send(part.at[lax.rem(lane_pos + d, GROUP)], part_in.at[d - 1], tensor_at(d))
        for d in range(1, GROUP)
    ]
    load_vact.wait()
    own = Projection(own_refs, 0)
    units = [Projection(unit_refs, n) for n in range(STEPS)]
    own.to_core(lax.dot_general(down_own[...], vact[...], NT, preferred_element_type=F32))
    for copy in part_moves:
        copy.wait_recv()
    summed = part[lane_pos]
    for d in range(GROUP - 1):
        summed = summed + part_in[d]
    share[...] = summed
    full[lane_pos] = summed
    full_moves = [send(share, full.at[lane_pos], tensor_at(d)) for d in range(1, GROUP)]

    down.step1()
    own.to_owners()

    stored = lax.broadcasted_iota(jnp.int32, (train, train), 0)
    hits = jnp.where(stored == index_ref[...], 1.0, 0.0).astype(BF16)
    counts = lax.dot_general(
        jnp.ones((8, train), BF16), hits, NT, preferred_element_type=F32
    )[0:1]

    load_cot.wait()
    for copy in full_moves:
        copy.wait_recv()
    proj = full[...].reshape(rank, train).astype(BF16).astype(F32)
    weighted = proj * counts
    high = weighted.astype(BF16)
    low = (weighted - high.astype(F32)).astype(BF16)
    product = jnp.dot(
        jnp.concatenate([high, low], axis=0), cot[...], preferred_element_type=F32
    )
    factor = ((product[:rank] + product[rank:]) * (-1.0 / train)).astype(BF16)
    for n, up in enumerate(ups):
        up.own[...] = factor[:, edges[n] : edges[n + 1]]
        up.step0()
    down.step2()
    down.wrap()

    def val_step(unit):
        rows = down_all[4 * unit : 4 * unit + 4].reshape(4 * rank, down_own.shape[1])
        units[unit].to_core(
            lax.dot_general(rows, vact[...], NT, preferred_element_type=F32)
        )

    def cot_dot(blocks):
        result = 0.0
        for n, rows in enumerate(blocks):
            result = result + lax.dot_general(
                rows, vcot[:, edges[n] : edges[n + 1]], NT, preferred_element_type=F32
            )
        return result

    def cot_step(unit):
        blocks = [
            up.held[4 * unit : 4 * unit + 4].reshape(4 * rank, up.own.shape[1]) for up in ups
        ]
        return units[unit].change(cot_dot(blocks))

    val_step(0)
    own.to_chips()
    down.step3()
    units[0].to_owners()
    for up in ups:
        up.step1()
    down.wrap2()
    val_step(1)
    units[0].to_chips()
    down.relay2()
    units[1].to_owners()
    for up in ups:
        up.step2()
    own.to_sibling()
    val_step(2)
    units[0].to_sibling()
    down.relay3()
    for up in ups:
        up.wrap()
    units[1].to_chips()
    units[2].to_owners()
    down.last()
    val_step(3)
    for up in ups:
        up.step3()
    load_vcot.wait()
    own_product = cot_dot([up.own[...] for up in ups])
    own_change = own.change(own_product)
    own_change = jnp.sum(own_change, axis=0, keepdims=True)
    units[3].to_owners()
    units[2].to_chips()
    units[1].to_sibling()
    for up in ups:
        up.wrap2()
    changes = [cot_step(0)]
    for up in ups:
        up.relay2()
    units[3].to_chips()
    units[2].to_sibling()
    changes.append(cot_step(1))
    for up in ups:
        up.relay3()
    units[3].to_sibling()
    changes.append(cot_step(2))
    for up in ups:
        up.last()
    changes.append(cot_step(3))

    own_mask = (label_ref[...] == me).astype(F32)
    other_mask = 1.0 - own_mask
    stack = jnp.concatenate(
        changes + [own_change, jnp.zeros((7, own_change.shape[1]), F32)], axis=0
    )
    own_part = jnp.sum(stack * own_mask, axis=1, keepdims=True)
    other_part = jnp.sum(stack * other_mask, axis=1, keepdims=True)

    row = lax.broadcasted_iota(jnp.int32, (24, 128), 0)
    column = lax.broadcasted_iota(jnp.int32, (24, 128), 1)

    def ring_column(d):
        return jnp.where(depth >= d, reach - d, 2 * reach - d)

    def far_column(p):
        return jnp.where(depth >= p, 2 * reach - p, reach - p)

    held_columns = (
        (ring_column(1), ring_column(7), far_column(0), far_column(8)),
        (ring_column(2), ring_column(6), far_column(1), far_column(7)),
        (ring_column(3), ring_column(5), far_column(2), far_column(6)),
        (ring_column(4), far_column(3), far_column(5), far_column(4)),
    )
    place = jnp.where(row == 4 * STEPS, reach, -1)
    for unit in range(STEPS):
        for n in range(4):
            place = jnp.where(row == 4 * unit + n, held_columns[unit][n], place)
    chosen = place == column
    own_row = jnp.sum(jnp.where(chosen, own_part, 0.0), axis=0, keepdims=True)
    other_row = jnp.sum(jnp.where(chosen, other_part, 0.0), axis=0, keepdims=True)
    top = row[:8]
    table[...] = jnp.where(top == 0, own_row, jnp.where(top == 1, other_row, 0.0))
    table_moves = [send(table, table_in.at[d - 1], tensor_at(d)) for d in range(1, GROUP)]
    own_count = jnp.maximum(jnp.sum(own_mask, axis=1, keepdims=True), 1.0)
    other_count = jnp.maximum(jnp.sum(other_mask, axis=1, keepdims=True), 1.0)
    for copy in table_moves:
        copy.wait_recv()
    result = jnp.zeros((8, 128), F32)
    for t in range(GROUP):
        away = lax.rem(lane_pos - t + GROUP, GROUP)
        theirs = table_in[lax.max(away - 1, 0)]
        result = result + jnp.where(away == 0, table[...], theirs)
    columns = own_out.shape[1]
    own_out[...] = result[0:1, :columns] / own_count
    other_out[...] = result[1:2, :columns] / other_count
    for copy in started:
        copy.wait_send()
    for when, copy in started_if:
        pl.when(when)(copy.wait_send)


def on_device(
    stored_inputs,
    stored_output_gradient,
    training_token_index,
    validation_inputs,
    validation_output_gradient,
    validation_row_skill,
    adapter_down_init,
):
    skills = lax.axis_size("skill")
    reach = skills // 8
    columns = 2 * reach + 1
    _, train, width = stored_inputs.shape
    hidden = stored_output_gradient.shape[2]
    rows = validation_inputs.shape[1]
    rank = adapter_down_init.shape[2]
    piece = rank // CORES
    cuts = [hidden // 128 * n // PIECES * 128 for n in range(PIECES + 1)]
    splits = [cuts[n + 1] - cuts[n] for n in range(PIECES)]
    share = rank // GROUP
    copies = (1 + PIECES) * 28 + 3 * (GROUP - 1) + (STEPS + 1) * 2 * CHIPS
    any_spec = pl.BlockSpec(memory_space=pl.ANY)
    vmem_spec = pl.BlockSpec(memory_space=pltpu.VMEM)
    return pl.pallas_call(
        functools.partial(kernel, skills, reach),
        out_shape=(
            jax.ShapeDtypeStruct((1, columns), F32),
            jax.ShapeDtypeStruct((1, columns), F32),
        ),
        in_specs=[any_spec, any_spec, vmem_spec, any_spec, any_spec, vmem_spec, any_spec],
        out_specs=(vmem_spec, vmem_spec),
        scratch_shapes=[
            pltpu.VMEM((train, width), BF16),
            pltpu.VMEM((train, hidden), BF16),
            pltpu.VMEM((rows, width), BF16),
            pltpu.VMEM((rows, hidden), BF16),
            pltpu.VMEM((rank, width), BF16),
            pltpu.VMEM((BLOCKS, rank, width), BF16),
            *[
                pltpu.VMEM(shape, BF16)
                for width_n in splits
                for shape in ((rank, width_n), (BLOCKS, rank, width_n))
            ],
            pltpu.VMEM((GROUP, rank // GROUP, train), F32),
            pltpu.VMEM((GROUP - 1, rank // GROUP, train), F32),
            pltpu.VMEM((rank // GROUP, train), F32),
            pltpu.VMEM((GROUP, rank // GROUP, train), F32),
            pltpu.VMEM((STEPS, CORES, CHIPS, piece, rows), F32),
            pltpu.VMEM((STEPS, CHIPS, piece, rows), F32),
            pltpu.VMEM((STEPS, CHIPS, piece, rows), BF16),
            pltpu.VMEM((STEPS, CHIPS - 1, piece, rows), BF16),
            pltpu.VMEM((STEPS, CORES, CHIPS, piece, rows), BF16),
            pltpu.VMEM((1, CORES, CHIPS, share, rows), F32),
            pltpu.VMEM((1, CHIPS, share, rows), F32),
            pltpu.VMEM((1, CHIPS, share, rows), F32),
            pltpu.VMEM((1, CHIPS - 1, share, rows), F32),
            pltpu.VMEM((1, CORES, CHIPS, share, rows), F32),
            pltpu.VMEM((8, 128), F32),
            pltpu.VMEM((GROUP - 1, 8, 128), F32),
            pltpu.SemaphoreType.DMA((5,)),
            pltpu.SemaphoreType.DMA((copies,)),
            pltpu.SemaphoreType.DMA((copies,)),
            pltpu.SemaphoreType.DMA(((1 + PIECES) * BLOCKS,)),
        ],
        compiler_params=pltpu.CompilerParams(
            collective_id=0, has_side_effects=True, vmem_limit_bytes=60 * 1024 * 1024
        ),
    )(
        stored_inputs[0],
        stored_output_gradient[0],
        training_token_index,
        validation_inputs[0],
        validation_output_gradient[0],
        validation_row_skill,
        jnp.swapaxes(adapter_down_init[0], 0, 1),
    )


def solution(mesh):
    in_specs = (
        P("skill", None, "tensor"),
        P("skill", None, "tensor"),
        P("skill", None),
        P("skill", None, "tensor"),
        P("skill", None, "tensor"),
        P("skill", None),
        P("skill", "tensor", None),
    )
    out_specs = (P("skill", None), P("skill", None))
    return jax.shard_map(
        on_device, mesh=mesh, in_specs=in_specs, out_specs=out_specs, check_vma=False
    )
```

```python
import functools

import jax
import jax.numpy as jnp
from jax import lax
from jax.experimental import pallas as pl
from jax.experimental.pallas import tpu as pltpu
from jax.sharding import PartitionSpec as P

F32 = jnp.float32
BF16 = jnp.bfloat16
STEPS = 4
BLOCKS = 17
PIECES = 2
CHIPS = 4
CORES = 2
GROUP = 8
LINE = 4
PASSING = 16
NT = (((1,), (1,)), ((), ()))


def kernel(
    skills,
    reach,
    act_hbm,
    cot_hbm,
    index_ref,
    vact_hbm,
    vcot_hbm,
    label_ref,
    down_hbm,
    deltas_out,
    act,
    cot,
    vact,
    vcot,
    down_own,
    down_all,
    up_own0,
    up_all0,
    up_own1,
    up_all1,
    part,
    part_in,
    share,
    full,
    unit_halves,
    unit_core_in,
    unit_out,
    unit_chip_in,
    unit_full,
    own_halves,
    own_core_in,
    own_out_f32,
    own_chip_in,
    own_full,
    table,
    table_in,
    load_sem,
    send_sem,
    recv_sem,
    block_sem,
):
    unit_refs = (unit_halves, unit_core_in, unit_out, unit_chip_in, unit_full)
    own_refs = (own_halves, own_core_in, own_out_f32, own_chip_in, own_full)
    me = lax.axis_index("skill")
    lane_pos = lax.axis_index("tensor")
    chip = lane_pos // CORES
    core = lax.rem(lane_pos, CORES)
    rank = down_own.shape[0]
    train = act.shape[0]
    piece = rank // CORES

    loads = []
    for n, (src, dst) in enumerate(
        [(down_hbm, down_own), (act_hbm, act), (vact_hbm, vact), (cot_hbm, cot), (vcot_hbm, vcot)]
    ):
        copy = pltpu.make_async_copy(src, dst, load_sem.at[n])
        copy.start()
        loads.append(copy)
    load_down, load_act, load_vact, load_cot, load_vcot = loads

    def skill_at(shift):
        return (lax.rem(me + shift + skills, skills), lane_pos)

    def tensor_at(shift):
        return (me, lax.rem(lane_pos + shift, GROUP))

    def chip_at(shift):
        return (me, lax.rem(chip + shift, CHIPS) * CORES + core)

    sibling = (me, chip * CORES + (1 - core))

    barrier = pltpu.get_barrier_semaphore()
    depth = lax.rem(me, reach)
    half = reach // 2
    low_half = depth < half
    line = lax.rem(me // reach, LINE)
    first_in_line = line == 0
    last_in_line = line == LINE - 1
    edge = (depth <= 1) | (depth >= reach - 2)
    middle = (depth == half) | (depth == half - 1)
    turning = (first_in_line & (depth == 0)) | (last_in_line & (depth == reach - 1))
    stepping = (first_in_line & (depth >= 1) & (depth <= half)) | (
        last_in_line & (depth >= half - 1) & (depth <= reach - 2)
    )
    onward = turning | stepping

    def ring_at(shift):
        return (me - depth + lax.rem(depth + shift + reach, reach), lane_pos)

    partners = [ring_at(1), ring_at(-1), skill_at(reach), skill_at(-reach)]
    partners += [tensor_at(d) for d in range(1, GROUP)]
    for partner in partners:
        pl.semaphore_signal(
            barrier, inc=1, device_id=partner, device_id_type=pl.DeviceIdType.MESH
        )

    started = []
    started_if = []

    def send(src, dst, target):
        n = len(started) + len(started_if)
        copy = pltpu.make_async_remote_copy(
            src_ref=src,
            dst_ref=dst,
            send_sem=send_sem.at[n],
            recv_sem=recv_sem.at[n],
            device_id=target,
            device_id_type=pl.DeviceIdType.MESH,
        )
        copy.start()
        started.append(copy)
        return copy

    class Stream:
        def __init__(self, own, held):
            self.own, self.held = own, held
            self.base = len(streams) * BLOCKS
            streams.append(self)

        def block(self, slot):
            return self.own if slot is None else self.held.at[slot]

        def send(self, source, slot, target, when=None):
            n = len(started) + len(started_if)
            copy = pltpu.make_async_remote_copy(
                src_ref=self.block(source),
                dst_ref=self.held.at[slot],
                send_sem=send_sem.at[n],
                recv_sem=block_sem.at[self.base + slot],
                device_id=target,
                device_id_type=pl.DeviceIdType.MESH,
            )
            if when is None:
                copy.start()
                started.append(copy)
            else:
                pl.when(when)(copy.start)
                started_if.append((when, copy))

        def wait(self, *slots):
            for slot in slots:
                pltpu.make_async_remote_copy(
                    src_ref=self.own,
                    dst_ref=self.held.at[slot],
                    send_sem=send_sem.at[0],
                    recv_sem=block_sem.at[self.base + slot],
                    device_id=sibling,
                    device_id_type=pl.DeviceIdType.MESH,
                ).wait_recv()

        def step0(self):
            self.send(None, 0, ring_at(1))
            self.send(None, 1, ring_at(-1))
            self.send(None, 2, skill_at(-reach))
            self.send(None, 3, skill_at(reach))

        def step1(self):
            self.wait(0, 1)
            self.send(0, 4, ring_at(1))
            self.send(1, 5, ring_at(-1))
            self.send(0, 6, skill_at(-reach), depth >= 1)
            self.send(1, 7, skill_at(reach), depth <= reach - 2)

        def step2(self):
            self.wait(4, 5)
            self.send(4, 8, ring_at(1))
            self.send(5, 9, ring_at(-1))
            self.send(
                4,
                10,
                skill_at(jnp.where(depth >= 2, -reach, reach)),
                jnp.where(depth >= 2, low_half | ~first_in_line, ~last_in_line),
            )
            self.send(
                5,
                11,
                skill_at(jnp.where(depth <= reach - 3, reach, -reach)),
                jnp.where(depth <= reach - 3, ~low_half | ~last_in_line, ~first_in_line),
            )

        def settle1(self):
            pl.when(~edge)(lambda: self.wait(2, 3))

        def settle2(self):
            pl.when(~onward)(lambda: self.wait(6, 7))

        def settle3(self):
            pl.when(~middle)(lambda: self.wait(jnp.where(low_half, 10, 11)))

        def wrap(self):
            pl.when(edge)(lambda: self.wait(2, 3))
            self.send(3, 6, ring_at(1), depth == reach - 1)
            self.send(2, 7, ring_at(-1), depth == 0)
            self.send(
                jnp.where(low_half, 2, 3),
                PASSING,
                ring_at(jnp.where(low_half, -1, 1)),
                (first_in_line & (depth == reach - 2)) | (last_in_line & (depth == 1)),
            )

        def wrap2(self):
            passing = (first_in_line & (depth == reach - 1)) | (last_in_line & (depth == 0))
            pl.when(passing)(lambda: self.wait(PASSING))
            self.send(
                PASSING,
                jnp.where(low_half, 11, 10),
                ring_at(jnp.where(low_half, -1, 1)),
                passing,
            )
            pl.when(onward)(lambda: self.wait(6, 7))
            self.send(
                jnp.where(low_half, 6, 7),
                jnp.where(low_half, 10, 11),
                ring_at(jnp.where(low_half, 1, -1)),
                turning,
            )
            self.send(
                jnp.where(first_in_line, 7, 6),
                jnp.where(first_in_line, 11, 10),
                ring_at(jnp.where(first_in_line, -1, 1)),
                stepping,
            )
        def relay2(self):
            near_slot, far_slot = jnp.where(low_half, 11, 10), jnp.where(low_half, 10, 11)
            self.wait(near_slot)
            self.send(
                near_slot,
                jnp.where(low_half, 14, 13),
                ring_at(jnp.where(low_half, -1, 1)),
                (depth >= 1) & (depth <= reach - 2),
            )
            pl.when(middle)(lambda: self.wait(far_slot))
            self.send(
                far_slot,
                jnp.where(low_half, 13, 14),
                ring_at(jnp.where(low_half, 1, -1)),
                middle,
            )

        def step3(self):
            self.wait(8, 9)
            self.send(8, 12, ring_at(1), lax.rem(depth + 1, reach) < half)
            self.send(9, 12, ring_at(-1), lax.rem(depth + reach - 1, reach) >= half)
            self.send(
                8,
                13,
                skill_at(jnp.where(depth == half - 1, -reach, reach)),
                low_half,
            )
            self.send(
                9,
                14,
                skill_at(jnp.where(depth == half, reach, -reach)),
                ~low_half,
            )

        def relay3(self):
            near_slot = jnp.where(low_half, 14, 13)
            self.wait(near_slot)
            self.send(
                near_slot,
                15,
                ring_at(jnp.where(low_half, -1, 1)),
                (depth >= 1) & (depth <= reach - 2),
            )
            pl.when(middle)(lambda: self.wait(jnp.where(low_half, 13, 14)))
            self.send(
                jnp.where(low_half, 13, 14), 15, ring_at(jnp.where(low_half, 1, -1)), middle
            )

        def last(self):
            self.wait(12, 15)
            pl.when((depth < half - 1) | (depth > half))(
                lambda: self.wait(jnp.where(low_half, 13, 14))
            )

    streams = []

    class Projection:
        def __init__(self, refs, index):
            self.halves, self.core_in, self.out, self.chip_in, self.full = [
                ref.at[index] for ref in refs
            ]

        def to_core(self, product):
            parts = product.reshape(CHIPS, CORES, -1, product.shape[1])
            for c in range(CORES):
                self.halves[c] = parts[:, c]
            self.move = send(self.halves.at[1 - core], self.core_in, sibling)

        def to_owners(self):
            self.move.wait_recv()
            both = self.halves[core] + self.core_in[...]
            self.out[...] = both.astype(self.out.dtype)
            self.core_in[...] = both
            self.moves = [
                send(
                    self.out.at[lax.rem(chip + d, CHIPS)], self.chip_in.at[d - 1], chip_at(d)
                )
                for d in range(1, CHIPS)
            ]

        def to_chips(self):
            value = self.core_in[chip]
            for d in range(CHIPS - 1):
                self.moves[d].wait_recv()
                value = value + self.chip_in[d].astype(F32)
            mine = self.full.at[core, chip]
            mine[...] = value.astype(self.full.dtype)
            self.moves = [send(mine, mine, chip_at(d)) for d in range(1, CHIPS)]

        def to_sibling(self):
            for move in self.moves:
                move.wait_recv()
            self.move = send(self.full.at[core], self.full.at[core], sibling)

        def change(self, product):
            self.move.wait_recv()
            parts = product.reshape(CHIPS, CORES, -1, product.shape[1])
            sums = []
            for c in range(CORES):
                sums.append(jnp.sum(parts[:, c] * self.full[c].astype(F32), axis=1))
            return sums[0] + sums[1]

    load_down.wait()
    load_act.wait()
    part[...] = lax.dot_general(
        down_own[...], act[...], NT, preferred_element_type=F32
    ).reshape(part.shape)
    pl.semaphore_wait(barrier, len(partners))
    down = Stream(down_own, down_all)
    ups = [Stream(*refs) for refs in ((up_own0, up_all0), (up_own1, up_all1))]
    edges = [0]
    for up in ups:
        edges.append(edges[-1] + up.own.shape[1])
    down.step0()

    part_moves = [
        send(part.at[lax.rem(lane_pos + d, GROUP)], part_in.at[d - 1], tensor_at(d))
        for d in range(1, GROUP)
    ]
    load_vact.wait()
    own = Projection(own_refs, 0)
    units = [Projection(unit_refs, n) for n in range(STEPS)]
    own.to_core(lax.dot_general(down_own[...], vact[...], NT, preferred_element_type=F32))
    for copy in part_moves:
        copy.wait_recv()
    summed = part[lane_pos]
    for d in range(GROUP - 1):
        summed = summed + part_in[d]
    share[...] = summed
    full[lane_pos] = summed
    full_moves = [send(share, full.at[lane_pos], tensor_at(d)) for d in range(1, GROUP)]

    down.step1()
    down.wrap()
    own.to_owners()

    stored = lax.broadcasted_iota(jnp.int32, (train, train), 0)
    hits = jnp.where(stored == index_ref[...], 1.0, 0.0).astype(BF16)
    counts = lax.dot_general(
        jnp.ones((8, train), BF16), hits, NT, preferred_element_type=F32
    )[0:1]

    load_cot.wait()
    for copy in full_moves:
        copy.wait_recv()
    proj = full[...].reshape(rank, train).astype(BF16).astype(F32)
    weighted = proj * counts
    high = weighted.astype(BF16)
    low = (weighted - high.astype(F32)).astype(BF16)
    product = jnp.dot(
        jnp.concatenate([high, low], axis=0), cot[...], preferred_element_type=F32
    )
    factor = ((product[:rank] + product[rank:]) * (-1.0 / train)).astype(BF16)
    for n, up in enumerate(ups):
        up.own[...] = factor[:, edges[n] : edges[n + 1]]
        up.step0()
    down.step2()
    down.wrap2()
    down.settle1()

    def val_step(unit):
        rows = down_all[4 * unit : 4 * unit + 4].reshape(4 * rank, down_own.shape[1])
        units[unit].to_core(
            lax.dot_general(rows, vact[...], NT, preferred_element_type=F32)
        )

    def cot_dot(blocks):
        result = 0.0
        for n, rows in enumerate(blocks):
            result = result + lax.dot_general(
                rows, vcot[:, edges[n] : edges[n + 1]], NT, preferred_element_type=F32
            )
        return result

    def cot_step(unit):
        blocks = [
            up.held[4 * unit : 4 * unit + 4].reshape(4 * rank, up.own.shape[1]) for up in ups
        ]
        return units[unit].change(cot_dot(blocks))

    val_step(0)
    own.to_chips()
    down.step3()
    units[0].to_owners()
    for up in ups:
        up.step1()
    down.relay2()
    for up in ups:
        up.wrap()
    down.settle2()
    val_step(1)
    units[0].to_chips()
    units[1].to_owners()
    for up in ups:
        up.step2()
    for up in ups:
        up.wrap2()
    down.relay3()
    own.to_sibling()
    down.settle3()
    val_step(2)
    units[0].to_sibling()
    units[1].to_chips()
    units[2].to_owners()
    for up in ups:
        up.step3()
    down.last()
    val_step(3)
    for up in ups:
        up.relay2()
    units[3].to_owners()
    units[2].to_chips()
    units[1].to_sibling()
    for up in ups:
        up.relay3()
    units[3].to_chips()
    units[2].to_sibling()
    load_vcot.wait()
    own_product = cot_dot([up.own[...] for up in ups])
    own_change = own.change(own_product)
    own_change = jnp.sum(own_change, axis=0, keepdims=True)
    for up in ups:
        up.settle1()
    changes = [cot_step(0)]
    for up in ups:
        up.settle2()
    changes.append(cot_step(1))
    units[3].to_sibling()
    for up in ups:
        up.settle3()
    changes.append(cot_step(2))
    for up in ups:
        up.last()
    changes.append(cot_step(3))

    own_mask = (label_ref[...] == me).astype(F32)
    other_mask = 1.0 - own_mask
    stack = jnp.concatenate(
        changes + [own_change, jnp.zeros((7, own_change.shape[1]), F32)], axis=0
    )
    own_part = jnp.sum(stack * own_mask, axis=1, keepdims=True)
    other_part = jnp.sum(stack * other_mask, axis=1, keepdims=True)

    row = lax.broadcasted_iota(jnp.int32, (24, 128), 0)
    column = lax.broadcasted_iota(jnp.int32, (24, 128), 1)

    def ring_column(d):
        return jnp.where(depth >= d, reach - d, 2 * reach - d)

    def far_column(p):
        return jnp.where(depth >= p, 2 * reach - p, reach - p)

    held_columns = (
        (ring_column(1), ring_column(7), far_column(0), far_column(8)),
        (ring_column(2), ring_column(6), far_column(1), far_column(7)),
        (ring_column(3), ring_column(5), far_column(2), far_column(6)),
        (ring_column(4), far_column(3), far_column(5), far_column(4)),
    )
    place = jnp.where(row == 4 * STEPS, reach, -1)
    for unit in range(STEPS):
        for n in range(4):
            place = jnp.where(row == 4 * unit + n, held_columns[unit][n], place)
    chosen = place == column
    own_row = jnp.sum(jnp.where(chosen, own_part, 0.0), axis=0, keepdims=True)
    other_row = jnp.sum(jnp.where(chosen, other_part, 0.0), axis=0, keepdims=True)
    top = row[:8]
    table[...] = jnp.where(top == 0, own_row, jnp.where(top == 1, other_row, 0.0))
    table_moves = [send(table, table_in.at[d - 1], tensor_at(d)) for d in range(1, GROUP)]
    own_count = jnp.maximum(jnp.sum(own_mask, axis=1, keepdims=True), 1.0)
    other_count = jnp.maximum(jnp.sum(other_mask, axis=1, keepdims=True), 1.0)
    for copy in table_moves:
        copy.wait_recv()
    result = jnp.zeros((8, 128), F32)
    for t in range(GROUP):
        away = lax.rem(lane_pos - t + GROUP, GROUP)
        theirs = table_in[lax.max(away - 1, 0)]
        result = result + jnp.where(away == 0, table[...], theirs)
    columns = deltas_out.shape[1]
    deltas_out[0:1] = result[0:1, :columns] / own_count
    deltas_out[1:2] = result[1:2, :columns] / other_count
    for copy in started:
        copy.wait_send()
    for when, copy in started_if:
        pl.when(when)(copy.wait_send)


def on_device(
    stored_inputs,
    stored_output_gradient,
    training_token_index,
    validation_inputs,
    validation_output_gradient,
    validation_row_skill,
    adapter_down_init,
):
    skills = lax.axis_size("skill")
    reach = skills // 8
    columns = 2 * reach + 1
    _, train, width = stored_inputs.shape
    hidden = stored_output_gradient.shape[2]
    rows = validation_inputs.shape[1]
    rank = adapter_down_init.shape[2]
    piece = rank // CORES
    cuts = [hidden // 128 * n // PIECES * 128 for n in range(PIECES + 1)]
    splits = [cuts[n + 1] - cuts[n] for n in range(PIECES)]
    share = rank // GROUP
    copies = (1 + PIECES) * 28 + 3 * (GROUP - 1) + (STEPS + 1) * 2 * CHIPS
    any_spec = pl.BlockSpec(memory_space=pl.ANY)
    vmem_spec = pl.BlockSpec(memory_space=pltpu.VMEM)
    deltas = pl.pallas_call(
        functools.partial(kernel, skills, reach),
        out_shape=jax.ShapeDtypeStruct((2, columns), F32),
        in_specs=[any_spec, any_spec, vmem_spec, any_spec, any_spec, vmem_spec, any_spec],
        out_specs=vmem_spec,
        scratch_shapes=[
            pltpu.VMEM((train, width), BF16),
            pltpu.VMEM((train, hidden), BF16),
            pltpu.VMEM((rows, width), BF16),
            pltpu.VMEM((rows, hidden), BF16),
            pltpu.VMEM((rank, width), BF16),
            pltpu.VMEM((BLOCKS, rank, width), BF16),
            *[
                pltpu.VMEM(shape, BF16)
                for width_n in splits
                for shape in ((rank, width_n), (BLOCKS, rank, width_n))
            ],
            pltpu.VMEM((GROUP, rank // GROUP, train), F32),
            pltpu.VMEM((GROUP - 1, rank // GROUP, train), F32),
            pltpu.VMEM((rank // GROUP, train), F32),
            pltpu.VMEM((GROUP, rank // GROUP, train), F32),
            pltpu.VMEM((STEPS, CORES, CHIPS, piece, rows), F32),
            pltpu.VMEM((STEPS, CHIPS, piece, rows), F32),
            pltpu.VMEM((STEPS, CHIPS, piece, rows), BF16),
            pltpu.VMEM((STEPS, CHIPS - 1, piece, rows), BF16),
            pltpu.VMEM((STEPS, CORES, CHIPS, piece, rows), BF16),
            pltpu.VMEM((1, CORES, CHIPS, share, rows), F32),
            pltpu.VMEM((1, CHIPS, share, rows), F32),
            pltpu.VMEM((1, CHIPS, share, rows), F32),
            pltpu.VMEM((1, CHIPS - 1, share, rows), F32),
            pltpu.VMEM((1, CORES, CHIPS, share, rows), F32),
            pltpu.VMEM((8, 128), F32),
            pltpu.VMEM((GROUP - 1, 8, 128), F32),
            pltpu.SemaphoreType.DMA((5,)),
            pltpu.SemaphoreType.DMA((copies,)),
            pltpu.SemaphoreType.DMA((copies,)),
            pltpu.SemaphoreType.DMA(((1 + PIECES) * BLOCKS,)),
        ],
        compiler_params=pltpu.CompilerParams(
            collective_id=0, has_side_effects=True, vmem_limit_bytes=60 * 1024 * 1024
        ),
    )(
        stored_inputs[0],
        stored_output_gradient[0],
        training_token_index,
        validation_inputs[0],
        validation_output_gradient[0],
        validation_row_skill,
        jnp.swapaxes(adapter_down_init[0], 0, 1),
    )
    return deltas[0:1], deltas[1:2]


def solution(mesh):
    in_specs = (
        P("skill", None, "tensor"),
        P("skill", None, "tensor"),
        P("skill", None),
        P("skill", None, "tensor"),
        P("skill", None, "tensor"),
        P("skill", None),
        P("skill", "tensor", None),
    )
    out_specs = (P("skill", None), P("skill", None))
    return jax.shard_map(
        on_device, mesh=mesh, in_specs=in_specs, out_specs=out_specs, check_vma=False
    )
```

```python
import functools

import jax
import jax.numpy as jnp
from jax import lax
from jax.experimental import pallas as pl
from jax.experimental.pallas import tpu as pltpu
from jax.sharding import PartitionSpec as P

F32 = jnp.float32
BF16 = jnp.bfloat16
STEPS = 4
BLOCKS = 17
PIECES = 2
CHIPS = 4
CORES = 2
GROUP = 8
LINE = 4
PASSING = 16
NT = (((1,), (1,)), ((), ()))


def kernel(
    skills,
    reach,
    act_hbm,
    cot_hbm,
    index_ref,
    vact_hbm,
    vcot_hbm,
    label_ref,
    down_hbm,
    deltas_out,
    act,
    cot,
    vact,
    vcot,
    down_own,
    down_all,
    up_own0,
    up_all0,
    up_own1,
    up_all1,
    part,
    part_in,
    share,
    full,
    unit_halves,
    unit_core_in,
    unit_out,
    unit_chip_in,
    unit_full,
    own_halves,
    own_core_in,
    own_out_f32,
    own_chip_in,
    own_full,
    table,
    table_in,
    load_sem,
    send_sem,
    recv_sem,
    block_sem,
):
    unit_refs = (unit_halves, unit_core_in, unit_out, unit_chip_in, unit_full)
    own_refs = (own_halves, own_core_in, own_out_f32, own_chip_in, own_full)
    me = lax.axis_index("skill")
    lane_pos = lax.axis_index("tensor")
    chip = lane_pos // CORES
    core = lax.rem(lane_pos, CORES)
    rank = down_own.shape[0]
    train = act.shape[0]
    piece = rank // CORES

    loads = []
    for n, (src, dst) in enumerate(
        [(down_hbm, down_own), (act_hbm, act), (vact_hbm, vact), (cot_hbm, cot), (vcot_hbm, vcot)]
    ):
        copy = pltpu.make_async_copy(src, dst, load_sem.at[n])
        copy.start()
        loads.append(copy)
    load_down, load_act, load_vact, load_cot, load_vcot = loads

    def skill_at(shift):
        return (lax.rem(me + shift + skills, skills), lane_pos)

    def tensor_at(shift):
        return (me, lax.rem(lane_pos + shift, GROUP))

    def chip_at(shift):
        return (me, lax.rem(chip + shift, CHIPS) * CORES + core)

    sibling = (me, chip * CORES + (1 - core))

    barrier = pltpu.get_barrier_semaphore()
    depth = lax.rem(me, reach)
    half = reach // 2
    low_half = depth < half
    line = lax.rem(me // reach, LINE)
    first_in_line = line == 0
    last_in_line = line == LINE - 1
    edge = (depth <= 1) | (depth >= reach - 2)
    middle = (depth == half) | (depth == half - 1)
    inner = (
        middle
        | (last_in_line & (depth == half - 2))
        | (first_in_line & (depth == half + 1))
    )
    turning = (first_in_line & (depth == 0)) | (last_in_line & (depth == reach - 1))
    stepping = (first_in_line & (depth >= 1) & (depth <= half)) | (
        last_in_line & (depth >= half - 1) & (depth <= reach - 2)
    )
    onward = turning | stepping

    def ring_at(shift):
        return (me - depth + lax.rem(depth + shift + reach, reach), lane_pos)

    partners = [ring_at(1), ring_at(-1), skill_at(reach), skill_at(-reach)]
    partners += [tensor_at(d) for d in range(1, GROUP)]
    for partner in partners:
        pl.semaphore_signal(
            barrier, inc=1, device_id=partner, device_id_type=pl.DeviceIdType.MESH
        )

    started = []
    started_if = []

    def send(src, dst, target):
        n = len(started) + len(started_if)
        copy = pltpu.make_async_remote_copy(
            src_ref=src,
            dst_ref=dst,
            send_sem=send_sem.at[n],
            recv_sem=recv_sem.at[n],
            device_id=target,
            device_id_type=pl.DeviceIdType.MESH,
        )
        copy.start()
        started.append(copy)
        return copy

    class Stream:
        def __init__(self, own, held):
            self.own, self.held = own, held
            self.base = len(streams) * BLOCKS
            streams.append(self)

        def block(self, slot):
            return self.own if slot is None else self.held.at[slot]

        def send(self, source, slot, target, when=None):
            n = len(started) + len(started_if)
            copy = pltpu.make_async_remote_copy(
                src_ref=self.block(source),
                dst_ref=self.held.at[slot],
                send_sem=send_sem.at[n],
                recv_sem=block_sem.at[self.base + slot],
                device_id=target,
                device_id_type=pl.DeviceIdType.MESH,
            )
            if when is None:
                copy.start()
                started.append(copy)
            else:
                pl.when(when)(copy.start)
                started_if.append((when, copy))

        def wait(self, *slots):
            for slot in slots:
                pltpu.make_async_remote_copy(
                    src_ref=self.own,
                    dst_ref=self.held.at[slot],
                    send_sem=send_sem.at[0],
                    recv_sem=block_sem.at[self.base + slot],
                    device_id=sibling,
                    device_id_type=pl.DeviceIdType.MESH,
                ).wait_recv()

        def step0(self):
            self.send(None, 0, ring_at(1))
            self.send(None, 1, ring_at(-1))
            self.send(None, 2, skill_at(-reach))
            self.send(None, 3, skill_at(reach))

        def step1(self):
            self.wait(0, 1)
            self.send(0, 4, ring_at(1))
            self.send(1, 5, ring_at(-1))
            self.send(0, 6, skill_at(-reach), depth >= 1)
            self.send(1, 7, skill_at(reach), depth <= reach - 2)

        def step2(self):
            self.wait(4, 5)
            self.send(4, 8, ring_at(1))
            self.send(5, 9, ring_at(-1))
            self.send(
                4,
                10,
                skill_at(jnp.where(depth >= 2, -reach, reach)),
                jnp.where(depth >= 2, low_half | ~first_in_line, ~last_in_line),
            )
            self.send(
                5,
                11,
                skill_at(jnp.where(depth <= reach - 3, reach, -reach)),
                jnp.where(depth <= reach - 3, ~low_half | ~last_in_line, ~first_in_line),
            )

        def settle1(self):
            pl.when(~edge)(lambda: self.wait(2, 3))

        def settle2(self):
            pl.when(~onward)(lambda: self.wait(6, 7))

        def settle3(self):
            pl.when(~inner)(lambda: self.wait(jnp.where(low_half, 10, 11)))

        def wrap(self):
            pl.when(edge)(lambda: self.wait(2, 3))
            self.send(3, 6, ring_at(1), depth == reach - 1)
            self.send(2, 7, ring_at(-1), depth == 0)
            self.send(
                jnp.where(low_half, 2, 3),
                PASSING,
                ring_at(jnp.where(low_half, -1, 1)),
                (first_in_line & (depth == reach - 2)) | (last_in_line & (depth == 1)),
            )

        def wrap2(self):
            passing = (first_in_line & (depth == reach - 1)) | (last_in_line & (depth == 0))
            pl.when(passing)(lambda: self.wait(PASSING))
            self.send(
                PASSING,
                jnp.where(low_half, 11, 10),
                ring_at(jnp.where(low_half, -1, 1)),
                passing,
            )
            pl.when(onward)(lambda: self.wait(6, 7))
            self.send(
                jnp.where(low_half, 6, 7),
                jnp.where(low_half, 10, 11),
                ring_at(jnp.where(low_half, 1, -1)),
                turning,
            )
            self.send(
                jnp.where(first_in_line, 7, 6),
                jnp.where(first_in_line, 11, 10),
                ring_at(jnp.where(first_in_line, -1, 1)),
                stepping,
            )
        def relay2(self):
            near_slot, far_slot = jnp.where(low_half, 11, 10), jnp.where(low_half, 10, 11)
            self.wait(near_slot)
            self.send(
                near_slot,
                jnp.where(low_half, 14, 13),
                ring_at(jnp.where(low_half, -1, 1)),
                (depth >= 1) & (depth <= reach - 2),
            )
            pl.when(inner)(lambda: self.wait(far_slot))
            self.send(
                far_slot,
                jnp.where(low_half, 13, 14),
                ring_at(jnp.where(low_half, 1, -1)),
                inner,
            )

        def step3(self):
            self.wait(8, 9)
            self.send(8, 12, ring_at(1), lax.rem(depth + 1, reach) < half)
            self.send(9, 12, ring_at(-1), lax.rem(depth + reach - 1, reach) >= half)
            self.send(
                8,
                13,
                skill_at(jnp.where(depth == half - 1, -reach, reach)),
                low_half & ((depth != half - 1) | ~first_in_line),
            )
            self.send(
                9,
                14,
                skill_at(jnp.where(depth == half, reach, -reach)),
                ~low_half & ((depth != half) | ~last_in_line),
            )

        def relay3(self):
            near_slot = jnp.where(low_half, 14, 13)
            self.wait(near_slot)
            self.send(
                near_slot,
                15,
                ring_at(jnp.where(low_half, -1, 1)),
                (depth >= 1) & (depth <= reach - 2),
            )
            pl.when(middle)(lambda: self.wait(jnp.where(low_half, 13, 14)))
            self.send(
                jnp.where(low_half, 13, 14), 15, ring_at(jnp.where(low_half, 1, -1)), middle
            )

        def last(self):
            self.wait(12, 15)
            pl.when((depth < half - 1) | (depth > half))(
                lambda: self.wait(jnp.where(low_half, 13, 14))
            )

    streams = []

    class Projection:
        def __init__(self, refs, index):
            self.halves, self.core_in, self.out, self.chip_in, self.full = [
                ref.at[index] for ref in refs
            ]

        def to_core(self, product):
            parts = product.reshape(CHIPS, CORES, -1, product.shape[1])
            for c in range(CORES):
                self.halves[c] = parts[:, c]
            self.move = send(self.halves.at[1 - core], self.core_in, sibling)

        def to_owners(self):
            self.move.wait_recv()
            both = self.halves[core] + self.core_in[...]
            self.out[...] = both.astype(self.out.dtype)
            self.core_in[...] = both
            self.moves = [
                send(
                    self.out.at[lax.rem(chip + d, CHIPS)], self.chip_in.at[d - 1], chip_at(d)
                )
                for d in range(1, CHIPS)
            ]

        def to_chips(self, direct=False):
            value = self.core_in[chip]
            for d in range(CHIPS - 1):
                self.moves[d].wait_recv()
                value = value + self.chip_in[d].astype(F32)
            mine = self.full.at[core, chip]
            mine[...] = value.astype(self.full.dtype)
            ways = (1, 2, 3) if direct else (1, 3)
            self.moves = [send(mine, mine, chip_at(d)) for d in ways]

        def to_far(self):
            cut = self.full.shape[2] // 2
            for n, (source, d) in enumerate(((3, 1), (1, 3))):
                self.moves[n].wait_recv()
                part = self.full.at[
                    core, lax.rem(chip + source, CHIPS), pl.ds(n * cut, cut)
                ]
                self.moves.append(send(part, part, chip_at(d)))
            self.moves = self.moves[2:]

        def to_sibling(self):
            for move in self.moves:
                move.wait_recv()
            self.move = send(self.full.at[core], self.full.at[core], sibling)

        def change(self, product):
            self.move.wait_recv()
            parts = product.reshape(CHIPS, CORES, -1, product.shape[1])
            sums = []
            for c in range(CORES):
                sums.append(jnp.sum(parts[:, c] * self.full[c].astype(F32), axis=1))
            return sums[0] + sums[1]

    load_down.wait()
    load_act.wait()
    part[...] = lax.dot_general(
        down_own[...], act[...], NT, preferred_element_type=F32
    ).reshape(part.shape)
    pl.semaphore_wait(barrier, len(partners))
    down = Stream(down_own, down_all)
    ups = [Stream(*refs) for refs in ((up_own0, up_all0), (up_own1, up_all1))]
    edges = [0]
    for up in ups:
        edges.append(edges[-1] + up.own.shape[1])
    down.step0()

    part_moves = [
        send(part.at[lax.rem(lane_pos + d, GROUP)], part_in.at[d - 1], tensor_at(d))
        for d in range(1, GROUP)
    ]
    load_vact.wait()
    own = Projection(own_refs, 0)
    units = [Projection(unit_refs, n) for n in range(STEPS)]
    own.to_core(lax.dot_general(down_own[...], vact[...], NT, preferred_element_type=F32))
    for copy in part_moves:
        copy.wait_recv()
    summed = part[lane_pos]
    for d in range(GROUP - 1):
        summed = summed + part_in[d]
    share[...] = summed
    full[lane_pos] = summed
    full_moves = [send(share, full.at[lane_pos], tensor_at(d)) for d in range(1, GROUP)]

    down.step1()
    down.wrap()
    own.to_owners()

    stored = lax.broadcasted_iota(jnp.int32, (train, train), 0)
    hits = jnp.where(stored == index_ref[...], 1.0, 0.0).astype(BF16)
    counts = lax.dot_general(
        jnp.ones((8, train), BF16), hits, NT, preferred_element_type=F32
    )[0:1]

    load_cot.wait()
    for copy in full_moves:
        copy.wait_recv()
    proj = full[...].reshape(rank, train).astype(BF16).astype(F32)
    weighted = proj * counts
    high = weighted.astype(BF16)
    low = (weighted - high.astype(F32)).astype(BF16)
    product = jnp.dot(
        jnp.concatenate([high, low], axis=0), cot[...], preferred_element_type=F32
    )
    factor = ((product[:rank] + product[rank:]) * (-1.0 / train)).astype(BF16)
    for n, up in enumerate(ups):
        up.own[...] = factor[:, edges[n] : edges[n + 1]]
        up.step0()
    down.step2()
    down.wrap2()
    down.settle1()

    def val_step(unit):
        rows = down_all[4 * unit : 4 * unit + 4].reshape(4 * rank, down_own.shape[1])
        units[unit].to_core(
            lax.dot_general(rows, vact[...], NT, preferred_element_type=F32)
        )

    def cot_dot(blocks):
        result = 0.0
        for n, rows in enumerate(blocks):
            result = result + lax.dot_general(
                rows, vcot[:, edges[n] : edges[n + 1]], NT, preferred_element_type=F32
            )
        return result

    def cot_step(unit):
        blocks = [
            up.held[4 * unit : 4 * unit + 4].reshape(4 * rank, up.own.shape[1]) for up in ups
        ]
        return units[unit].change(cot_dot(blocks))

    val_step(0)
    own.to_chips(True)
    down.step3()
    units[0].to_owners()
    for up in ups:
        up.step1()
    down.relay2()
    for up in ups:
        up.wrap()
    down.settle2()
    val_step(1)
    units[0].to_chips()
    units[1].to_owners()
    for up in ups:
        up.step2()
    for up in ups:
        up.wrap2()
    down.relay3()
    own.to_sibling()
    down.settle3()
    val_step(2)
    units[0].to_far()
    units[1].to_chips()
    units[2].to_owners()
    for up in ups:
        up.step3()
    down.last()
    val_step(3)
    for up in ups:
        up.relay2()
    units[3].to_owners()
    units[2].to_chips()
    units[1].to_far()
    units[0].to_sibling()
    for up in ups:
        up.relay3()
    units[3].to_chips()
    units[2].to_far()
    units[1].to_sibling()
    load_vcot.wait()
    own_product = cot_dot([up.own[...] for up in ups])
    own_change = own.change(own_product)
    own_change = jnp.sum(own_change, axis=0, keepdims=True)
    for up in ups:
        up.settle1()
    changes = [cot_step(0)]
    for up in ups:
        up.settle2()
    changes.append(cot_step(1))
    units[3].to_far()
    units[2].to_sibling()
    for up in ups:
        up.settle3()
    changes.append(cot_step(2))
    for up in ups:
        up.last()
    units[3].to_sibling()
    changes.append(cot_step(3))

    own_mask = (label_ref[...] == me).astype(F32)
    other_mask = 1.0 - own_mask
    stack = jnp.concatenate(
        changes + [own_change, jnp.zeros((7, own_change.shape[1]), F32)], axis=0
    )
    own_part = jnp.sum(stack * own_mask, axis=1, keepdims=True)
    other_part = jnp.sum(stack * other_mask, axis=1, keepdims=True)

    row = lax.broadcasted_iota(jnp.int32, (24, 128), 0)
    column = lax.broadcasted_iota(jnp.int32, (24, 128), 1)

    def ring_column(d):
        return jnp.where(depth >= d, reach - d, 2 * reach - d)

    def far_column(p):
        return jnp.where(depth >= p, 2 * reach - p, reach - p)

    held_columns = (
        (ring_column(1), ring_column(7), far_column(0), far_column(8)),
        (ring_column(2), ring_column(6), far_column(1), far_column(7)),
        (ring_column(3), ring_column(5), far_column(2), far_column(6)),
        (ring_column(4), far_column(3), far_column(5), far_column(4)),
    )
    place = jnp.where(row == 4 * STEPS, reach, -1)
    for unit in range(STEPS):
        for n in range(4):
            place = jnp.where(row == 4 * unit + n, held_columns[unit][n], place)
    chosen = place == column
    own_row = jnp.sum(jnp.where(chosen, own_part, 0.0), axis=0, keepdims=True)
    other_row = jnp.sum(jnp.where(chosen, other_part, 0.0), axis=0, keepdims=True)
    top = row[:8]
    table[...] = jnp.where(top == 0, own_row, jnp.where(top == 1, other_row, 0.0))
    table_moves = [send(table, table_in.at[d - 1], tensor_at(d)) for d in range(1, GROUP)]
    own_count = jnp.maximum(jnp.sum(own_mask, axis=1, keepdims=True), 1.0)
    other_count = jnp.maximum(jnp.sum(other_mask, axis=1, keepdims=True), 1.0)
    for copy in table_moves:
        copy.wait_recv()
    result = jnp.zeros((8, 128), F32)
    for t in range(GROUP):
        away = lax.rem(lane_pos - t + GROUP, GROUP)
        theirs = table_in[lax.max(away - 1, 0)]
        result = result + jnp.where(away == 0, table[...], theirs)
    columns = deltas_out.shape[1]
    deltas_out[0:1] = result[0:1, :columns] / own_count
    deltas_out[1:2] = result[1:2, :columns] / other_count
    for copy in started:
        copy.wait_send()
    for when, copy in started_if:
        pl.when(when)(copy.wait_send)


def on_device(
    stored_inputs,
    stored_output_gradient,
    training_token_index,
    validation_inputs,
    validation_output_gradient,
    validation_row_skill,
    adapter_down_init,
):
    skills = lax.axis_size("skill")
    reach = skills // 8
    columns = 2 * reach + 1
    _, train, width = stored_inputs.shape
    hidden = stored_output_gradient.shape[2]
    rows = validation_inputs.shape[1]
    rank = adapter_down_init.shape[2]
    piece = rank // CORES
    cuts = [hidden // 128 * n // PIECES * 128 for n in range(PIECES + 1)]
    splits = [cuts[n + 1] - cuts[n] for n in range(PIECES)]
    share = rank // GROUP
    copies = (1 + PIECES) * 28 + 3 * (GROUP - 1) + (STEPS + 1) * (2 * CHIPS + 1)
    any_spec = pl.BlockSpec(memory_space=pl.ANY)
    vmem_spec = pl.BlockSpec(memory_space=pltpu.VMEM)
    deltas = pl.pallas_call(
        functools.partial(kernel, skills, reach),
        out_shape=jax.ShapeDtypeStruct((2, columns), F32),
        in_specs=[any_spec, any_spec, vmem_spec, any_spec, any_spec, vmem_spec, any_spec],
        out_specs=vmem_spec,
        scratch_shapes=[
            pltpu.VMEM((train, width), BF16),
            pltpu.VMEM((train, hidden), BF16),
            pltpu.VMEM((rows, width), BF16),
            pltpu.VMEM((rows, hidden), BF16),
            pltpu.VMEM((rank, width), BF16),
            pltpu.VMEM((BLOCKS, rank, width), BF16),
            *[
                pltpu.VMEM(shape, BF16)
                for width_n in splits
                for shape in ((rank, width_n), (BLOCKS, rank, width_n))
            ],
            pltpu.VMEM((GROUP, rank // GROUP, train), F32),
            pltpu.VMEM((GROUP - 1, rank // GROUP, train), F32),
            pltpu.VMEM((rank // GROUP, train), F32),
            pltpu.VMEM((GROUP, rank // GROUP, train), F32),
            pltpu.VMEM((STEPS, CORES, CHIPS, piece, rows), F32),
            pltpu.VMEM((STEPS, CHIPS, piece, rows), F32),
            pltpu.VMEM((STEPS, CHIPS, piece, rows), BF16),
            pltpu.VMEM((STEPS, CHIPS - 1, piece, rows), BF16),
            pltpu.VMEM((STEPS, CORES, CHIPS, piece, rows), BF16),
            pltpu.VMEM((1, CORES, CHIPS, share, rows), F32),
            pltpu.VMEM((1, CHIPS, share, rows), F32),
            pltpu.VMEM((1, CHIPS, share, rows), F32),
            pltpu.VMEM((1, CHIPS - 1, share, rows), F32),
            pltpu.VMEM((1, CORES, CHIPS, share, rows), F32),
            pltpu.VMEM((8, 128), F32),
            pltpu.VMEM((GROUP - 1, 8, 128), F32),
            pltpu.SemaphoreType.DMA((5,)),
            pltpu.SemaphoreType.DMA((copies,)),
            pltpu.SemaphoreType.DMA((copies,)),
            pltpu.SemaphoreType.DMA(((1 + PIECES) * BLOCKS,)),
        ],
        compiler_params=pltpu.CompilerParams(
            collective_id=0, has_side_effects=True, vmem_limit_bytes=60 * 1024 * 1024
        ),
    )(
        stored_inputs[0],
        stored_output_gradient[0],
        training_token_index,
        validation_inputs[0],
        validation_output_gradient[0],
        validation_row_skill,
        jnp.swapaxes(adapter_down_init[0], 0, 1),
    )
    return deltas[0:1], deltas[1:2]


def solution(mesh):
    in_specs = (
        P("skill", None, "tensor"),
        P("skill", None, "tensor"),
        P("skill", None),
        P("skill", None, "tensor"),
        P("skill", None, "tensor"),
        P("skill", None),
        P("skill", "tensor", None),
    )
    out_specs = (P("skill", None), P("skill", None))
    return jax.shard_map(
        on_device, mesh=mesh, in_specs=in_specs, out_specs=out_specs, check_vma=False
    )
```
